1024 devices in a mesh: row: 32 (over x, z_hi), grp: 16 (over y, z_lo), col: 2 (over core).
Axes of the slice: x: 8, y: 8, z: 8 (z_hi: 4, z_lo: 2; z = z_hi * 2 + z_lo), core: 2. Of those that a mesh axis runs over, the one named last changes fastest.
Arguments:
- state: float32 [512, 512, 256], P('row', ('grp', 'col')), may hold values from -6 to 6
- rate: float32 [512, 512], P('row', ('grp', 'col')), may hold values from 0.02 to 0.24
- cotangent: bfloat16 [512, 512, 256], P('row', ('grp', 'col')), may hold values from -6 to 6
- dest: int32 [32, 32, 256, 1], P('row', ('grp', 'col')), may hold values from 0 to 15; in each aligned block of 256 rows (0 to 255, 256 to 511, ..., all dimensions but the last counted through in order) at most 32 rows name the same one
- w_in: bfloat16 [16, 256, 1024], P('grp'), may hold values from -0.375 to 0.375
- w_out: bfloat16 [16, 256, 1024], P('grp'), may hold values from -0.1875 to 0.1875
Outputs:
- new_state: float32 [512, 512, 256], P('row', ('grp', 'col'))
- column_adjoint: bfloat16 [512, 512, 256], P('row', ('grp', 'col'))
- weight_grads: float32 [16, 4096, 128], P('grp', ('row', 'col'))
The draws below stay inside these ranges and needn't reach their ends.
Inputs may be any that keep to these rules, and one draw needn't show every extreme that they name: `dest`: within one block no owner receives more than 32 columns, and some owner receives exactly 32 in some block.
All inputs are finite; a program needn't handle non-finite values.
Results may differ from the reference program's by a relative error of at most 0.0053.
Values may be sent and summed in bfloat16 or wider, within the bound.
A program may use at most 32 MiB of HBM per device.

```python
import math
import jax
import jax.numpy as jnp
import numpy as np
from jax import lax

FIELDS = 8
LEV = 32
HID = 1024
BX = 16
BY = 16
STEPS = 4
CAP = 32
EXPERTS = 16
NX = 512
NY = 512
FLAT = 4096
N_ROW = 32
N_GRP = 16
N_COL = 2


def levels(stream_key, shape, cuts, least, largest):
    loudness, own = 1.0, jax.random.fold_in(stream_key, 6)
    for dim, parts in cuts:
        draws = jnp.exp(jax.random.uniform(jax.random.fold_in(own, dim), (parts,), jnp.float32, least / len(cuts), largest / len(cuts)))
        loudness = loudness * jnp.repeat(draws, shape[dim] // parts).reshape([-1 if axis == dim else 1 for axis in range(len(shape))])
    return loudness


def assign_block(key, own, number, rows, count, top, most, slope):
    ranking = jax.random.permutation(key, count)
    heavy_load, common = shares(count, rows * top, most, slope, True), shares(count, rows * top, most, slope, False)
    places = jnp.arange(count)

    def named(lengths, offset_by):
        used = int((lengths > 0).sum())
        fixed = max(1, used // 4)
        moved = fixed + (places - fixed + offset_by * (used - fixed)) % max(1, count - fixed)
        return jnp.zeros((count,), jnp.int32).at[ranking[jnp.where(places < fixed, places, moved)]].set(jnp.asarray(lengths, jnp.int32))

    lengths = jnp.where(number % 4 == 0, named(heavy_load, number // 4), named(common, number - number // 4 - 1))
    mixed = jax.random.permutation(jax.random.fold_in(own, 3), count)
    source_of, sink = mixed[0:count // 2 * 2:2], mixed[1:count // 2 * 2:2]
    margin = jnp.minimum(lengths[source_of] - 1, most - lengths[sink]) // 2
    margin = jnp.where((source_of == ranking[0]) | (sink == ranking[0]) | (lengths[sink] == 0), 0, jnp.maximum(margin, 0))
    moved = jax.random.randint(jax.random.fold_in(own, 4), (count // 2,), 0, 1 << 20) % (margin + 1)
    lengths = lengths.at[source_of].add(-moved).at[sink].add(moved)
    members = jnp.searchsorted(jnp.cumsum(lengths), jnp.arange(rows * top), side="right").astype(jnp.int32)
    table = members.reshape(top, rows).T
    table = table[jax.random.permutation(jax.random.fold_in(own, 1), rows)]
    offset_by = jax.random.randint(jax.random.fold_in(own, 2), (rows, 1), 0, top)
    return jnp.take_along_axis(table, (jnp.arange(top)[None, :] + offset_by) % top, axis=1)


def shares(count, total, most, skew, full):
    weights = [(1 << 20) // math.isqrt(rank ** skew) + 1 for rank in range(1, count + 1)]
    largest = most if full else min(most, max(-(-total // count), total * weights[0] // sum(weights)))
    least = 1 if total - largest >= count - 1 else 0
    holding, rest = [largest] + [least] * (count - 1), total - largest - least * (count - 1)
    while rest > 0:
        free = [i for i in range(1, count) if holding[i] < largest] or [i for i in range(1, count) if holding[i] < most]
        whole, remaining = sum([weights[i] for i in free]), rest
        for i in free:
            addition = min(most - holding[i], max(1, remaining * weights[i] // whole), rest)
            holding[i] = holding[i] + addition
            rest = rest - addition
    return np.array(holding)


def gaussian(stream_key, shape, spread, reach, shards=(), kind=jnp.bfloat16):
    array = jax.random.normal(stream_key, shape, jnp.float32) * spread
    if len(shards) > 0:
        array = levels(stream_key, shape, shards, -0.22, 0.18) * array
    return jnp.clip(array, min=-reach, max=reach).astype(kind)


def setup_inputs(seed: int = 0) -> dict:
    keys = jax.random.split(jax.random.key(seed), 7)
    state = gaussian(keys[0], (NX, NY, FIELDS * LEV), 1.0, 6.0, ((0, 32), (1, 32)), jnp.float32)
    rate = jnp.clip(jnp.exp(math.log(0.24) - 2.4849066 * jax.random.uniform(keys[1], (NX, NY), jnp.float32) ** levels(keys[1], (NX, NY), ((0, 32), (1, 32)), -0.2, 0.2)), 0.02, 0.24)
    cotangent = gaussian(keys[2], (NX, NY, FIELDS * LEV), 1.0, 6.0, ((0, 32), (1, 32)))
    dest_keys = jax.random.split(jax.random.fold_in(keys[3], 1), N_ROW * (N_GRP * N_COL) * (BX * BY) // (BX * BY))
    dest_turns = jax.random.permutation(jax.random.fold_in(keys[3], 3), N_ROW * (N_GRP * N_COL) * (BX * BY) // (BX * BY))
    dest = jax.vmap(lambda own, number: assign_block(jax.random.fold_in(keys[3], 2), own, number, BX * BY, N_GRP, 1, 2 * BX * BY // N_GRP, 2))(dest_keys, dest_turns).reshape((N_ROW, N_GRP * N_COL, BX * BY, 1))
    w_in = gaussian(keys[4], (EXPERTS, FIELDS * LEV, HID), (FIELDS * LEV) ** -0.5, 0.375, ((0, 16),))
    w_out = gaussian(keys[5], (EXPERTS, FIELDS * LEV, HID), HID ** -0.5, 0.1875, ((0, 16),))
    return dict(state=state, rate=rate, cotangent=cotangent, dest=dest, w_in=w_in, w_out=w_out)


def silu_slope(value):
    logistic = jax.nn.sigmoid(value)
    return logistic * (1.0 + value * (1.0 - logistic))


def reference(state, rate, cotangent, dest, w_in, w_out):
    feats = FIELDS * LEV
    field = state
    for step in range(STEPS):
        beside = jnp.roll(field, 1, 0) + jnp.roll(field, -1, 0) + jnp.roll(field, 1, 1) + jnp.roll(field, -1, 1)
        field = field + rate[:, :, None] * (beside - 4.0 * field)

    def to_groups(grid):
        shaped = grid.reshape(N_ROW, BX, N_GRP, N_COL, BY, feats)
        shaped = shaped.transpose(0, 3, 2, 1, 4, 5)
        return shaped.reshape(N_ROW * N_COL, N_GRP, BX * BY, feats)

    def from_groups(groups):
        shaped = groups.reshape(N_ROW, N_COL, N_GRP, BX, BY, feats)
        shaped = shaped.transpose(0, 3, 2, 1, 4, 5)
        return shaped.reshape(N_ROW * BX, N_GRP * N_COL * BY, feats)

    columns = to_groups(state.astype(jnp.bfloat16))
    cotans = to_groups(cotangent)
    routes = dest.reshape(N_ROW, N_GRP, N_COL, BX * BY).transpose(0, 2, 1, 3).reshape(N_ROW * N_COL, N_GRP, BX * BY)
    onehot = (routes[..., None] == jnp.arange(N_GRP, dtype=jnp.int32)).astype(jnp.int32)
    ranks = jnp.cumsum(onehot, axis=2) - 1
    slots = jnp.sum(ranks * onehot, axis=-1)
    places = (routes * CAP + slots).astype(jnp.int32)
    w_in32 = w_in.astype(jnp.float32)
    w_out32 = w_out.astype(jnp.float32)

    def pack_one(rows, where):
        return jnp.zeros((N_GRP * CAP, feats), rows.dtype).at[where].set(rows)

    def group_step(carry, pieces):
        group_cols, group_cots, group_places = pieces
        packed_cols = jax.vmap(pack_one)(group_cols, group_places)
        packed_cots = jax.vmap(pack_one)(group_cots, group_places)
        owner_cols = packed_cols.reshape(N_GRP, N_GRP, CAP, feats).transpose(1, 0, 2, 3).reshape(N_GRP, N_GRP * CAP, feats)
        owner_cots = packed_cots.reshape(N_GRP, N_GRP, CAP, feats).transpose(1, 0, 2, 3).reshape(N_GRP, N_GRP * CAP, feats)
        cols32 = owner_cols.astype(jnp.float32)
        pre = jnp.einsum("erf,efh->erh", cols32, w_in32)
        act = jax.nn.silu(pre).astype(jnp.bfloat16)
        act32 = act.astype(jnp.float32)
        tend = jnp.einsum("erh,efh->erf", act32, w_out32).astype(jnp.bfloat16)
        dtend = (0.5 * owner_cots.astype(jnp.float32)).astype(jnp.bfloat16)
        dtend32 = dtend.astype(jnp.float32)
        dact = jnp.einsum("erf,efh->erh", dtend32, w_out32)
        dpre = (dact * silu_slope(pre)).astype(jnp.bfloat16)
        dpre32 = dpre.astype(jnp.float32)
        adjoint = jnp.einsum("erh,efh->erf", dpre32, w_in32).astype(jnp.bfloat16)
        grad_in = jnp.einsum("erf,erh->efh", cols32, dpre32)
        grad_out = jnp.einsum("erf,erh->efh", dtend32, act32)
        carry = carry + jnp.stack([grad_in, grad_out], axis=1)

        def unpack(owner_rows):
            by_source = owner_rows.reshape(N_GRP, N_GRP, CAP, feats).transpose(1, 0, 2, 3).reshape(N_GRP, N_GRP * CAP, feats)
            return jax.vmap(lambda rows, where: jnp.take(rows, where, axis=0))(by_source, group_places)

        return carry, (unpack(tend), unpack(adjoint))

    start = jnp.zeros((N_GRP, 2, feats, HID), jnp.float32)
    grads, (tends, adjoints) = lax.scan(group_step, start, (columns, cotans, places))
    tendency = from_groups(tends)
    column_adjoint = from_groups(adjoints)
    new_state = field + 0.5 * tendency.astype(jnp.float32)
    weight_grads = grads.reshape(N_GRP, FLAT, 128)
    return new_state, column_adjoint, weight_grads
```

```python
import jax
import jax.numpy as jnp
from jax import lax
from jax.experimental import pallas as pl
from jax.experimental.pallas import tpu as pltpu
from jax.sharding import PartitionSpec as P

F32, BF16, I32 = jnp.float32, jnp.bfloat16, jnp.int32
MESH = pl.DeviceIdType.MESH

STEPS = 4
SIDE = 16
FEATS = 256
HID = 1024
CAP = 32
ROWS, BLOCKS = 32, 32
NX, NZ = 8, 4
NY, NL = 8, 2
SLOTS = NY * NL
COLUMNS = SIDE * SIDE
WIDE = FEATS + 128
XF = 640
TN = 256

OFFSETS = sorted(
    ((dy, dl) for dy in range(NY) for dl in range(NL)),
    key=lambda o: 4 * ((4 - min(o[0], 8 - o[0])) % 4) + 2 * (o[0] >= 4) + o[1],
)
SENDING = [2, 3, 1] + list(range(4, SLOTS))
SIDES = [(0, 1), (0, -1), (1, 0), (-1, 0), (1, 1), (1, -1), (-1, 1), (-1, -1)]
FAR_X = [4, 3, 5, 2, 6, 1, 7]
FAR_Z = [2, 1, 3]


def iota(shape, dim):
    return lax.broadcasted_iota(I32, shape, dim)


def kernel(
    state_ref,
    rate_ref,
    cot_ref,
    dest_ref,
    win_hbm,
    wout_hbm,
    new_ref,
    adj_ref,
    grad_ref,
    win,
    wout,
    send,
    recv,
    back,
    home,
    places_ref,
    act_ref,
    dpre_ref,
    edge,
    halo,
    field_a,
    field_b,
    rates,
    grads,
    pair,
    half,
    x1,
    z1,
    sum_x,
    out_x,
    z2,
    sum_z,
    out_z,
    x2,
    w_sem,
    fwd_send,
    fwd_recv,
    back_send,
    back_recv,
    edge_send,
    edge_recv,
    pair_send,
    pair_recv,
    x1_send,
    x1_recv,
    z1_send,
    z1_recv,
    x2_send,
    x2_recv,
    z2_send,
    z2_recv,
):
    row, grp, col = lax.axis_index("row"), lax.axis_index("grp"), lax.axis_index("col")
    x, z = row // NZ, row % NZ
    y, l = grp // NL, grp % NL
    block = grp * 2 + col

    def at_expert(dy, dl):
        return {"row": row, "grp": ((y + dy) % NY) * NL + (l + dl) % NL, "col": col}

    def at_source(dy, dl):
        return {"row": row, "grp": ((y + NY - dy) % NY) * NL + (l + dl) % NL, "col": col}

    def at_side(di, dj):
        there = (block + dj + BLOCKS) % BLOCKS
        return {"row": (row + di + ROWS) % ROWS, "grp": there // 2, "col": there % 2}

    def at_x(dx):
        return {"row": ((x + dx) % NX) * NZ + z, "grp": grp, "col": col}

    def at_z(dz):
        return {"row": x * NZ + (z + dz) % NZ, "grp": grp, "col": col}

    partner = {"row": row, "grp": grp, "col": 1 - col}

    barrier = pltpu.get_barrier_semaphore()
    greeted = (
        [at_expert(*OFFSETS[t]) for t in SENDING]
        + [at_side(*o) for o in SIDES]
        + [at_x(dx) for dx in FAR_X]
        + [at_z(dz) for dz in FAR_Z]
        + [partner]
    )
    for there in greeted:
        pl.semaphore_signal(barrier, inc=1, device_id=there, device_id_type=MESH)

    def remote(src, dst, sent, came, there):
        return pltpu.make_async_remote_copy(
            src_ref=src, dst_ref=dst, send_sem=sent, recv_sem=came, device_id=there, device_id_type=MESH
        )

    w_copies = [
        pltpu.make_async_copy(win_hbm, win, w_sem.at[0]),
        pltpu.make_async_copy(wout_hbm, wout, w_sem.at[1]),
    ]
    for copy in w_copies:
        copy.start()

    dest = dest_ref[...]
    dy = ((dest >> 1) - y) & (NY - 1)
    dl = (dest & 1) ^ l
    slot = ((4 - jnp.minimum(dy, NY - dy)) & 3) * 4 + jnp.where(dy >= 4, 2, 0) + dl
    chosen = jnp.where(iota((SLOTS, COLUMNS), 0) == slot, 1.0, 0.0)
    upto = jnp.where(
        iota((COLUMNS, COLUMNS), 0) <= iota((COLUMNS, COLUMNS), 1), 1.0, 0.0
    ).astype(BF16)
    ranks = jnp.dot(chosen.astype(BF16), upto, preferred_element_type=F32)
    rank = jnp.sum(chosen * ranks, axis=0, keepdims=True) - 1.0
    places = slot.astype(F32) * CAP + rank
    places_ref[...] = places
    placing = jnp.where(
        iota((SLOTS * CAP, COLUMNS), 0) == places.astype(I32), 1.0, 0.0
    ).astype(BF16)
    cells = state_ref[...].astype(BF16)
    packed = jnp.dot(placing, cells.reshape(COLUMNS, FEATS), preferred_element_type=F32)
    packed = packed.astype(BF16).reshape(SLOTS, CAP, FEATS)
    send[:, :, 0:FEATS] = packed
    recv[0, :, 0:FEATS] = packed[0]
    packed = 0.5 * jnp.dot(
        placing, cot_ref[...].reshape(COLUMNS, FEATS), preferred_element_type=F32
    )
    packed = packed.astype(BF16).reshape(SLOTS, CAP, FEATS)
    send[:, :, FEATS:] = packed
    recv[0, :, FEATS:] = packed[0]

    edge[:, :, :, 0:FEATS] = cells.reshape(SIDE, 2, 8, FEATS)
    diagonal = iota((SIDE, SIDE), 0) == iota((SIDE, SIDE), 1)
    for i in range(SIDE):
        line = jnp.broadcast_to(rate_ref[i : i + 1, :], (SIDE, SIDE))
        line = jnp.sum(jnp.where(diagonal, line, 0.0), axis=1, keepdims=True)
        line = jnp.broadcast_to(line, (SIDE, 128))
        rates[4 + i, 8 : 8 + SIDE, :] = line
        edge[i, :, :, FEATS:] = line.astype(BF16).reshape(2, 8, 128)

    pl.semaphore_wait(barrier, len(greeted))

    fwd = {
        t: remote(send.at[t], recv.at[t], fwd_send.at[t], fwd_recv.at[t], at_expert(*OFFSETS[t]))
        for t in SENDING
    }
    for t in SENDING:
        fwd[t].start()

    span = {-1: (slice(0, 4), slice(20, 24)), 1: (slice(12, 16), slice(0, 4)), 0: (slice(0, 16), slice(4, 20))}
    tile = {-1: (slice(0, 1), slice(3, 4)), 1: (slice(1, 2), slice(0, 1)), 0: (slice(0, 2), slice(1, 3))}
    edges = [
        remote(
            edge.at[span[di][0], tile[dj][0]],
            halo.at[span[di][1], tile[dj][1]],
            edge_send.at[n],
            edge_recv.at[n],
            at_side(di, dj),
        )
        for n, (di, dj) in enumerate(SIDES)
    ]
    for copy in edges:
        copy.start()

    for copy in w_copies:
        copy.wait()

    homeward = {
        t: remote(back.at[t], home.at[t], back_send.at[t], back_recv.at[t], at_source(*OFFSETS[t]))
        for t in SENDING
    }
    for g in range(4):
        for t in range(4 * g, 4 * g + 4):
            if t:
                fwd[t].wait_recv()
        lines = slice(128 * g, 128 * g + 128)
        came = recv[4 * g : 4 * g + 4].reshape(128, 2 * FEATS)
        columns, dtend = came[:, 0:FEATS], came[:, FEATS:]
        for h in range(0, HID, TN):
            pre = jnp.dot(columns, win[:, h : h + TN], preferred_element_type=F32)
            dact = jnp.dot(dtend, wout[:, h : h + TN], preferred_element_type=F32)
            sigma = 1.0 / (1.0 + jnp.exp(-pre))
            act_ref[lines, h : h + TN] = (pre * sigma).astype(BF16)
            slope = sigma * (1.0 + pre * (1.0 - sigma))
            dpre_ref[lines, h : h + TN] = (dact * slope).astype(BF16)
        across = (((1,), (1,)), ((), ()))
        tend = lax.dot_general(act_ref[lines, :], wout[...], across, preferred_element_type=F32)
        adjoint = lax.dot_general(dpre_ref[lines, :], win[...], across, preferred_element_type=F32)
        tend = tend.astype(BF16).reshape(4, CAP, FEATS)
        adjoint = adjoint.astype(BF16).reshape(4, CAP, FEATS)
        back[4 * g : 4 * g + 4, :, 0:FEATS] = tend
        back[4 * g : 4 * g + 4, :, FEATS:] = adjoint
        if g == 0:
            home[0, :, 0:FEATS] = tend[0]
            home[0, :, FEATS:] = adjoint[0]
        for t in range(4 * g, 4 * g + 4):
            if t:
                homeward[t].start()

    pairs = []
    for n, (first, hidden) in enumerate(((FEATS, act_ref), (0, dpre_ref))):
        left = recv[:, :, first : first + FEATS].reshape(SLOTS * CAP, FEATS)
        out = slice(16 - 16 * n, 32 - 16 * n)
        for h in range(0, HID, TN):
            part = lax.dot_general(
                left, hidden[:, h : h + TN], (((0,), (0,)), ((), ())), preferred_element_type=F32
            )
            grads[out, :, :, h : h + TN] = part.reshape(16, 2, 8, TN)
        copy = remote(grads.at[out, 1 - col], pair.at[out], pair_send.at[n], pair_recv.at[n], partner)
        copy.start()
        pairs.append(copy)
    for n, copy in enumerate(pairs):
        copy.wait_recv()
        out = slice(16 - 16 * n, 32 - 16 * n)
        both = grads[out, col] + pair[out]
        half[4 - 4 * n : 8 - 4 * n] = both.astype(BF16).reshape(4, NZ, 8, HID)

    first_x = [
        remote(
            half.at[(x + dx) % NX, :, :, 0:XF], x1.at[dx], x1_send.at[dx], x1_recv.at[dx], at_x(dx)
        )
        for dx in FAR_X
    ]
    first_z = [
        remote(
            half.at[:, (z + dz) % NZ, :, XF:], z1.at[dz], z1_send.at[dz], z1_recv.at[dz], at_z(dz)
        )
        for dz in FAR_Z
    ]
    for copy in first_x + first_z:
        copy.start()

    for copy in edges:
        copy.wait_recv()
    for top in (0, 20):
        cells = halo[top : top + 4].astype(F32).reshape(4, 32, WIDE)
        field_a[top : top + 4] = cells[:, :, 0:FEATS]
        rates[top : top + 4] = cells[:, :, FEATS:]
    for t in (0, 3):
        cells = halo[4:20, t].astype(F32)
        field_a[4:20, 8 * t : 8 * t + 8] = cells[:, :, 0:FEATS]
        rates[4:20, 8 * t : 8 * t + 8] = cells[:, :, FEATS:]
    field_a[4:20, 8:24] = state_ref[...]
    old, new = field_a, field_b
    for step in range(1, STEPS + 1):

        def advance(n, carry, old=old, new=new, step=step):
            i = step + 2 * n
            here = old[pl.ds(i, 2)]
            beside = old[pl.ds(i - 1, 2)] + old[pl.ds(i + 1, 2)]
            beside = beside + pltpu.roll(here, 1, 1) + pltpu.roll(here, 31, 1)
            pace = rates[pl.ds(i, 2)]
            pace = jnp.concatenate([pace, pace], axis=2)
            new[pl.ds(i, 2)] = here + pace * (beside - 4.0 * here)
            return carry

        lax.fori_loop(0, 12 - step, advance, 0)
        old, new = new, old

    for copy in first_x:
        copy.wait_recv()
    total = half[x, :, :, 0:XF].astype(F32)
    for dx in range(1, NX):
        total = total + x1[dx].astype(F32)
    sum_x[...] = total
    out_x[...] = total.astype(BF16)
    last_z = [
        remote(out_x.at[(z + dz) % NZ], z2.at[dz], z2_send.at[dz], z2_recv.at[dz], at_z(dz)) for dz in FAR_Z
    ]
    for copy in last_z:
        copy.start()
    for copy in first_z:
        copy.wait_recv()
    total = half[:, z, :, XF:].astype(F32)
    for dz in range(1, NZ):
        total = total + z1[dz].astype(F32)
    sum_z[...] = total
    out_z[...] = total.astype(BF16)
    last_x = [
        remote(out_z.at[(x + dx) % NX], x2.at[dx], x2_send.at[dx], x2_recv.at[dx], at_x(dx)) for dx in FAR_X
    ]
    for copy in last_x:
        copy.start()

    for t in SENDING:
        homeward[t].wait_recv()
    square = iota((COLUMNS, COLUMNS), 0) == iota((COLUMNS, COLUMNS), 1)
    tall = jnp.where(square, jnp.broadcast_to(places_ref[...], (COLUMNS, COLUMNS)), 0.0)
    tall = jnp.sum(tall, axis=1, keepdims=True).astype(I32)
    picking = jnp.where(iota((COLUMNS, SLOTS * CAP), 1) == tall, 1.0, 0.0).astype(BF16)
    tend = jnp.dot(
        picking, home[:, :, 0:FEATS].reshape(SLOTS * CAP, FEATS), preferred_element_type=F32
    )
    new_ref[...] = old[4:20, 8:24] + 0.5 * tend.reshape(SIDE, SIDE, FEATS)
    adjoint = jnp.dot(
        picking, home[:, :, FEATS:].reshape(SLOTS * CAP, FEATS), preferred_element_type=F32
    )
    adj_ref[...] = adjoint.astype(BF16).reshape(SIDE, SIDE, FEATS)

    for copy in last_z:
        copy.wait_recv()
    total = sum_x[z]
    for dz in range(1, NZ):
        total = total + z2[dz].astype(F32)
    for h in range(0, XF, 128):
        grad_ref[pl.ds(h // 128, 8, stride=8), :] = total[:, h : h + 128]
    for copy in last_x:
        copy.wait_recv()
    total = sum_z[x]
    for dx in range(1, NX):
        total = total + x2[dx].astype(F32)
    for h in range(XF, HID, 128):
        grad_ref[pl.ds(h // 128, 8, stride=8), :] = total[:, h - XF : h - XF + 128]

    for t in SENDING:
        fwd[t].wait_send()
        homeward[t].wait_send()
    for copy in edges + pairs + first_x + first_z + last_x + last_z:
        copy.wait_send()


def local(state, rate, cotangent, dest, w_in, w_out):
    vmem = pl.BlockSpec(memory_space=pltpu.VMEM)
    hbm = pl.BlockSpec(memory_space=pl.ANY)
    sems = pltpu.SemaphoreType.DMA
    new_state, adjoint, grads = pl.pallas_call(
        kernel,
        out_shape=(
            jax.ShapeDtypeStruct((SIDE, SIDE, FEATS), F32),
            jax.ShapeDtypeStruct((SIDE, SIDE, FEATS), BF16),
            jax.ShapeDtypeStruct((HID // 128 * 8, 128), F32),
        ),
        in_specs=[vmem, vmem, vmem, vmem, hbm, hbm],
        out_specs=(vmem, vmem, vmem),
        scratch_shapes=[
            pltpu.VMEM((FEATS, HID), BF16),
            pltpu.VMEM((FEATS, HID), BF16),
            pltpu.VMEM((SLOTS, CAP, 2 * FEATS), BF16),
            pltpu.VMEM((SLOTS, CAP, 2 * FEATS), BF16),
            pltpu.VMEM((SLOTS, CAP, 2 * FEATS), BF16),
            pltpu.VMEM((SLOTS, CAP, 2 * FEATS), BF16),
            pltpu.VMEM((1, COLUMNS), F32),
            pltpu.VMEM((SLOTS * CAP, HID), BF16),
            pltpu.VMEM((SLOTS * CAP, HID), BF16),
            pltpu.VMEM((SIDE, 2, 8, WIDE), BF16),
            pltpu.VMEM((24, 4, 8, WIDE), BF16),
            pltpu.VMEM((24, 32, FEATS), F32),
            pltpu.VMEM((24, 32, FEATS), F32),
            pltpu.VMEM((24, 32, 128), F32),
            pltpu.VMEM((32, 2, 8, HID), F32),
            pltpu.VMEM((32, 8, HID), F32),
            pltpu.VMEM((NX, NZ, 8, HID), BF16),
            pltpu.VMEM((NX, NZ, 8, XF), BF16),
            pltpu.VMEM((NZ, NX, 8, HID - XF), BF16),
            pltpu.VMEM((NZ, 8, XF), F32),
            pltpu.VMEM((NZ, 8, XF), BF16),
            pltpu.VMEM((NZ, 8, XF), BF16),
            pltpu.VMEM((NX, 8, HID - XF), F32),
            pltpu.VMEM((NX, 8, HID - XF), BF16),
            pltpu.VMEM((NX, 8, HID - XF), BF16),
            sems((2,)),
            sems((SLOTS,)),
            sems((SLOTS,)),
            sems((SLOTS,)),
            sems((SLOTS,)),
            sems((8,)),
            sems((8,)),
            sems((2,)),
            sems((2,)),
            sems((NX,)),
            sems((NX,)),
            sems((NZ,)),
            sems((NZ,)),
            sems((NX,)),
            sems((NX,)),
            sems((NZ,)),
            sems((NZ,)),
        ],
        compiler_params=pltpu.CompilerParams(collective_id=0, has_side_effects=True),
        name="window",
    )(state, rate, cotangent, dest.reshape(1, COLUMNS), w_in[0], w_out[0])
    return new_state, adjoint, grads[None]


def solution(mesh):
    in_specs = (
        P("row", ("grp", "col"), None),
        P("row", ("grp", "col")),
        P("row", ("grp", "col"), None),
        P("row", ("grp", "col"), None, None),
        P("grp", None, None),
        P("grp", None, None),
    )
    out_specs = (
        P("row", ("grp", "col"), None),
        P("row", ("grp", "col"), None),
        P("grp", ("row", "col"), None),
    )
    return jax.shard_map(local, mesh=mesh, in_specs=in_specs, out_specs=out_specs, check_vma=False)
```

```python
import jax
import jax.numpy as jnp
from jax import lax
from jax.experimental import pallas as pl
from jax.experimental.pallas import tpu as pltpu
from jax.sharding import PartitionSpec as P

F32, BF16, I32 = jnp.float32, jnp.bfloat16, jnp.int32
MESH = pl.DeviceIdType.MESH

STEPS = 4
SIDE = 16
FEATS = 256
HID = 1024
CAP = 32
ROWS, BLOCKS = 32, 32
NX, NZ = 8, 4
NY, NL = 8, 2
SLOTS = NY * NL
COLUMNS = SIDE * SIDE
WIDE = FEATS + 128
XF = 640
TN = 256

OFFSETS = sorted(
    ((dy, dl) for dy in range(NY) for dl in range(NL)),
    key=lambda o: 4 * ((4 - min(o[0], 8 - o[0])) % 4) + 2 * (o[0] >= 4) + o[1],
)
SENDING = [2, 3, 1] + list(range(4, SLOTS))
SIDES = [(0, 1), (0, -1), (1, 0), (-1, 0), (1, 1), (1, -1), (-1, 1), (-1, -1)]
FAR_X = [4, 3, 5, 2, 6, 1, 7]
FAR_Z = [2, 1, 3]
PAIR = BF16


def iota(shape, dim):
    return lax.broadcasted_iota(I32, shape, dim)


def kernel(
    state_hbm,
    rate_hbm,
    cot_hbm,
    dest_hbm,
    win_hbm,
    wout_hbm,
    new_ref,
    adj_ref,
    grad_ref,
    state_ref,
    rate_ref,
    cot_ref,
    dest_ref,
    win,
    wout,
    send,
    recv,
    back,
    home,
    places_ref,
    act_ref,
    dpre_ref,
    edge,
    halo,
    field_a,
    field_b,
    rates,
    grads,
    pair,
    half,
    x1,
    z1,
    sum_x,
    out_x,
    z2,
    sum_z,
    out_z,
    x2,
    in_sem,
    fwd_send,
    fwd_recv,
    back_send,
    back_recv,
    edge_send,
    edge_recv,
    pair_send,
    pair_recv,
    x1_send,
    x1_recv,
    z1_send,
    z1_recv,
    x2_send,
    x2_recv,
    z2_send,
    z2_recv,
):
    row, grp, col = lax.axis_index("row"), lax.axis_index("grp"), lax.axis_index("col")
    x, z = row // NZ, row % NZ
    y, l = grp // NL, grp % NL
    block = grp * 2 + col

    def at_expert(dy, dl):
        return {"row": row, "grp": ((y + dy) % NY) * NL + (l + dl) % NL, "col": col}

    def at_source(dy, dl):
        return {"row": row, "grp": ((y + NY - dy) % NY) * NL + (l + dl) % NL, "col": col}

    def at_side(di, dj):
        there = (block + dj + BLOCKS) % BLOCKS
        return {"row": (row + di + ROWS) % ROWS, "grp": there // 2, "col": there % 2}

    def at_x(dx):
        return {"row": ((x + dx) % NX) * NZ + z, "grp": grp, "col": col}

    def at_z(dz):
        return {"row": x * NZ + (z + dz) % NZ, "grp": grp, "col": col}

    partner = {"row": row, "grp": grp, "col": 1 - col}

    barrier = pltpu.get_barrier_semaphore()
    greeted = (
        [at_expert(*OFFSETS[t]) for t in SENDING]
        + [at_side(*o) for o in SIDES]
        + [at_x(dx) for dx in FAR_X]
        + [at_z(dz) for dz in FAR_Z]
        + [partner]
    )
    for there in greeted:
        pl.semaphore_signal(barrier, inc=1, device_id=there, device_id_type=MESH)

    def remote(src, dst, sent, came, there):
        return pltpu.make_async_remote_copy(
            src_ref=src, dst_ref=dst, send_sem=sent, recv_sem=came, device_id=there, device_id_type=MESH
        )

    loads = [
        pltpu.make_async_copy(src, dst, in_sem.at[n])
        for n, (src, dst) in enumerate(
            (
                (dest_hbm, dest_ref),
                (state_hbm, state_ref),
                (cot_hbm, cot_ref),
                (rate_hbm, rate_ref),
                (win_hbm, win),
                (wout_hbm, wout),
            )
        )
    ]
    for copy in loads:
        copy.start()
    loads[0].wait()

    dest = dest_ref[...]
    dy = ((dest >> 1) - y) & (NY - 1)
    dl = (dest & 1) ^ l
    slot = ((4 - jnp.minimum(dy, NY - dy)) & 3) * 4 + jnp.where(dy >= 4, 2, 0) + dl
    chosen = jnp.where(iota((SLOTS, COLUMNS), 0) == slot, 1.0, 0.0)
    upto = jnp.where(
        iota((COLUMNS, COLUMNS), 0) <= iota((COLUMNS, COLUMNS), 1), 1.0, 0.0
    ).astype(BF16)
    ranks = jnp.dot(chosen.astype(BF16), upto, preferred_element_type=F32)
    rank = jnp.sum(chosen * ranks, axis=0, keepdims=True) - 1.0
    places = slot.astype(F32) * CAP + rank
    places_ref[...] = places
    placing = jnp.where(
        iota((SLOTS * CAP, COLUMNS), 0) == places.astype(I32), 1.0, 0.0
    ).astype(BF16)
    loads[1].wait()
    cells = state_ref[...].astype(BF16)
    packed = jnp.dot(placing, cells.reshape(COLUMNS, FEATS), preferred_element_type=F32)
    packed = packed.astype(BF16).reshape(SLOTS, CAP, FEATS)
    send[:, :, 0:FEATS] = packed
    recv[0, :, 0:FEATS] = packed[0]
    loads[2].wait()
    packed = 0.5 * jnp.dot(
        placing, cot_ref[...].reshape(COLUMNS, FEATS), preferred_element_type=F32
    )
    packed = packed.astype(BF16).reshape(SLOTS, CAP, FEATS)
    send[:, :, FEATS:] = packed
    recv[0, :, FEATS:] = packed[0]

    pl.semaphore_wait(barrier, len(greeted))

    fwd = {
        t: remote(send.at[t], recv.at[t], fwd_send.at[t], fwd_recv.at[t], at_expert(*OFFSETS[t]))
        for t in SENDING
    }
    for t in SENDING[:3]:
        fwd[t].start()

    loads[3].wait()
    edge[:, :, :, 0:FEATS] = cells.reshape(SIDE, 2, 8, FEATS)
    diagonal = iota((SIDE, SIDE), 0) == iota((SIDE, SIDE), 1)
    for i in range(SIDE):
        line = jnp.broadcast_to(rate_ref[i : i + 1, :], (SIDE, SIDE))
        line = jnp.sum(jnp.where(diagonal, line, 0.0), axis=1, keepdims=True)
        line = jnp.broadcast_to(line, (SIDE, 128))
        rates[4 + i, 8 : 8 + SIDE, :] = line
        edge[i, :, :, FEATS:] = line.astype(BF16).reshape(2, 8, 128)

    span = {-1: (slice(0, 4), slice(20, 24)), 1: (slice(12, 16), slice(0, 4)), 0: (slice(0, 16), slice(4, 20))}
    tile = {-1: (slice(0, 1), slice(3, 4)), 1: (slice(1, 2), slice(0, 1)), 0: (slice(0, 2), slice(1, 3))}
    edges = [
        remote(
            edge.at[span[di][0], tile[dj][0]],
            halo.at[span[di][1], tile[dj][1]],
            edge_send.at[n],
            edge_recv.at[n],
            at_side(di, dj),
        )
        for n, (di, dj) in enumerate(SIDES)
    ]
    for copy in edges:
        copy.start()
    for t in SENDING[3:]:
        fwd[t].start()

    for copy in loads[4:]:
        copy.wait()

    homeward = {
        t: remote(back.at[t], home.at[t], back_send.at[t], back_recv.at[t], at_source(*OFFSETS[t]))
        for t in SENDING
    }
    for g in range(4):
        for t in range(4 * g, 4 * g + 4):
            if t:
                fwd[t].wait_recv()
        if g == 3:
            for t in SENDING[:11]:
                homeward[t].start()
        lines = slice(128 * g, 128 * g + 128)
        came = recv[4 * g : 4 * g + 4].reshape(128, 2 * FEATS)
        columns, dtend = came[:, 0:FEATS], came[:, FEATS:]
        for h in range(0, HID, TN):
            pre = jnp.dot(columns, win[:, h : h + TN], preferred_element_type=F32)
            dact = jnp.dot(dtend, wout[:, h : h + TN], preferred_element_type=F32)
            sigma = 1.0 / (1.0 + jnp.exp(-pre))
            act_ref[lines, h : h + TN] = (pre * sigma).astype(BF16)
            slope = sigma * (1.0 + pre * (1.0 - sigma))
            dpre_ref[lines, h : h + TN] = (dact * slope).astype(BF16)
        across = (((1,), (1,)), ((), ()))
        tend = lax.dot_general(act_ref[lines, :], wout[...], across, preferred_element_type=F32)
        adjoint = lax.dot_general(dpre_ref[lines, :], win[...], across, preferred_element_type=F32)
        tend = tend.astype(BF16).reshape(4, CAP, FEATS)
        adjoint = adjoint.astype(BF16).reshape(4, CAP, FEATS)
        back[4 * g : 4 * g + 4, :, 0:FEATS] = tend
        back[4 * g : 4 * g + 4, :, FEATS:] = adjoint
        if g == 0:
            home[0, :, 0:FEATS] = tend[0]
            home[0, :, FEATS:] = adjoint[0]
        if g == 3:
            for t in SENDING[11:]:
                homeward[t].start()

        if g == 1:
            for copy in edges:
                copy.wait_recv()
            for top in (0, 20):
                cells = halo[top : top + 4].astype(F32).reshape(4, 32, WIDE)
                field_a[top : top + 4] = cells[:, :, 0:FEATS]
                rates[top : top + 4] = cells[:, :, FEATS:]
            for t in (0, 3):
                cells = halo[4:20, t].astype(F32)
                field_a[4:20, 8 * t : 8 * t + 8] = cells[:, :, 0:FEATS]
                rates[4:20, 8 * t : 8 * t + 8] = cells[:, :, FEATS:]
            field_a[4:20, 8:24] = state_ref[...]
            old, new = field_a, field_b
            for step in range(1, STEPS + 1):

                def advance(n, carry, old=old, new=new, step=step):
                    i = step + 2 * n
                    here = old[pl.ds(i, 2)]
                    beside = old[pl.ds(i - 1, 2)] + old[pl.ds(i + 1, 2)]
                    beside = beside + pltpu.roll(here, 1, 1) + pltpu.roll(here, 31, 1)
                    pace = rates[pl.ds(i, 2)]
                    pace = jnp.concatenate([pace, pace], axis=2)
                    new[pl.ds(i, 2)] = here + pace * (beside - 4.0 * here)
                    return carry

                lax.fori_loop(0, 12 - step, advance, 0)
                old, new = new, old

    parts = (slice(0, XF), slice(XF, HID))
    pairs = []
    for n, part in enumerate(parts):
        for first, hidden, out in ((FEATS, act_ref, slice(16, 32)), (0, dpre_ref, slice(0, 16))):
            left = recv[:, :, first : first + FEATS].reshape(SLOTS * CAP, FEATS)
            for h in range(part.start, part.stop, TN):
                width = min(TN, part.stop - h)
                piece = lax.dot_general(
                    left, hidden[:, h : h + width], (((0,), (0,)), ((), ())), preferred_element_type=F32
                )
                grads[out, :, :, h : h + width] = piece.reshape(16, 2, 8, width).astype(PAIR)
        copy = remote(
            grads.at[:, 1 - col, :, part], pair.at[:, :, part], pair_send.at[n], pair_recv.at[n], partner
        )
        copy.start()
        pairs.append(copy)
    first_x = [
        remote(
            half.at[(x + dx) % NX, :, :, 0:XF], x1.at[dx], x1_send.at[dx], x1_recv.at[dx], at_x(dx)
        )
        for dx in FAR_X
    ]
    first_z = [
        remote(
            half.at[:, (z + dz) % NZ, :, XF:], z1.at[dz], z1_send.at[dz], z1_recv.at[dz], at_z(dz)
        )
        for dz in FAR_Z
    ]
    for part, copy, onward in zip(parts, pairs, (first_x, first_z)):
        copy.wait_recv()
        both = grads[:, col, :, part].astype(F32) + pair[:, :, part].astype(F32)
        half[:, :, :, part] = both.astype(BF16).reshape(NX, NZ, 8, part.stop - part.start)
        for there in onward:
            there.start()

    for copy in first_x:
        copy.wait_recv()
    total = half[x, :, :, 0:XF].astype(F32)
    for dx in range(1, NX):
        total = total + x1[dx].astype(F32)
    sum_x[...] = total
    out_x[...] = total.astype(BF16)
    last_z = [
        remote(out_x.at[(z + dz) % NZ], z2.at[dz], z2_send.at[dz], z2_recv.at[dz], at_z(dz)) for dz in FAR_Z
    ]
    for copy in last_z:
        copy.start()
    for copy in first_z:
        copy.wait_recv()
    total = half[:, z, :, XF:].astype(F32)
    for dz in range(1, NZ):
        total = total + z1[dz].astype(F32)
    sum_z[...] = total
    out_z[...] = total.astype(BF16)
    last_x = [
        remote(out_z.at[(x + dx) % NX], x2.at[dx], x2_send.at[dx], x2_recv.at[dx], at_x(dx)) for dx in FAR_X
    ]
    for copy in last_x:
        copy.start()

    for t in SENDING:
        homeward[t].wait_recv()
    square = iota((COLUMNS, COLUMNS), 0) == iota((COLUMNS, COLUMNS), 1)
    tall = jnp.where(square, jnp.broadcast_to(places_ref[...], (COLUMNS, COLUMNS)), 0.0)
    tall = jnp.sum(tall, axis=1, keepdims=True).astype(I32)
    picking = jnp.where(iota((COLUMNS, SLOTS * CAP), 1) == tall, 1.0, 0.0).astype(BF16)
    tend = jnp.dot(
        picking, home[:, :, 0:FEATS].reshape(SLOTS * CAP, FEATS), preferred_element_type=F32
    )
    new_ref[...] = old[4:20, 8:24] + 0.5 * tend.reshape(SIDE, SIDE, FEATS)
    adjoint = jnp.dot(
        picking, home[:, :, FEATS:].reshape(SLOTS * CAP, FEATS), preferred_element_type=F32
    )
    adj_ref[...] = adjoint.astype(BF16).reshape(SIDE, SIDE, FEATS)

    for copy in last_z:
        copy.wait_recv()
    total = sum_x[z]
    for dz in range(1, NZ):
        total = total + z2[dz].astype(F32)
    for h in range(0, XF, 128):
        grad_ref[pl.ds(h // 128, 8, stride=8), :] = total[:, h : h + 128]
    for copy in last_x:
        copy.wait_recv()
    total = sum_z[x]
    for dx in range(1, NX):
        total = total + x2[dx].astype(F32)
    for h in range(XF, HID, 128):
        grad_ref[pl.ds(h // 128, 8, stride=8), :] = total[:, h - XF : h - XF + 128]

    for t in SENDING:
        fwd[t].wait_send()
        homeward[t].wait_send()
    for copy in edges + pairs + first_x + first_z + last_x + last_z:
        copy.wait_send()


def put_out(*refs):
    copies = [pltpu.make_async_copy(refs[n], refs[3 + n], refs[6].at[n]) for n in range(3)]
    for copy in copies:
        copy.start()
    for copy in copies:
        copy.wait()


def local(state, rate, cotangent, dest, w_in, w_out):
    vmem = pl.BlockSpec(memory_space=pltpu.VMEM)
    hbm = pl.BlockSpec(memory_space=pl.ANY)
    sems = pltpu.SemaphoreType.DMA
    results = pl.pallas_call(
        kernel,
        out_shape=(
            pltpu.VMEM((SIDE, SIDE, FEATS), F32),
            pltpu.VMEM((SIDE, SIDE, FEATS), BF16),
            pltpu.VMEM((HID // 128 * 8, 128), F32),
        ),
        in_specs=[hbm] * 6,
        out_specs=(vmem, vmem, vmem),
        scratch_shapes=[
            pltpu.VMEM((SIDE, SIDE, FEATS), F32),
            pltpu.VMEM((SIDE, SIDE), F32),
            pltpu.VMEM((SIDE, SIDE, FEATS), BF16),
            pltpu.VMEM((1, COLUMNS), I32),
            pltpu.VMEM((FEATS, HID), BF16),
            pltpu.VMEM((FEATS, HID), BF16),
            pltpu.VMEM((SLOTS, CAP, 2 * FEATS), BF16),
            pltpu.VMEM((SLOTS, CAP, 2 * FEATS), BF16),
            pltpu.VMEM((SLOTS, CAP, 2 * FEATS), BF16),
            pltpu.VMEM((SLOTS, CAP, 2 * FEATS), BF16),
            pltpu.VMEM((1, COLUMNS), F32),
            pltpu.VMEM((SLOTS * CAP, HID), BF16),
            pltpu.VMEM((SLOTS * CAP, HID), BF16),
            pltpu.VMEM((SIDE, 2, 8, WIDE), BF16),
            pltpu.VMEM((24, 4, 8, WIDE), BF16),
            pltpu.VMEM((24, 32, FEATS), F32),
            pltpu.VMEM((24, 32, FEATS), F32),
            pltpu.VMEM((24, 32, 128), F32),
            pltpu.VMEM((32, 2, 8, HID), PAIR),
            pltpu.VMEM((32, 8, HID), PAIR),
            pltpu.VMEM((NX, NZ, 8, HID), BF16),
            pltpu.VMEM((NX, NZ, 8, XF), BF16),
            pltpu.VMEM((NZ, NX, 8, HID - XF), BF16),
            pltpu.VMEM((NZ, 8, XF), F32),
            pltpu.VMEM((NZ, 8, XF), BF16),
            pltpu.VMEM((NZ, 8, XF), BF16),
            pltpu.VMEM((NX, 8, HID - XF), F32),
            pltpu.VMEM((NX, 8, HID - XF), BF16),
            pltpu.VMEM((NX, 8, HID - XF), BF16),
            sems((6,)),
            sems((SLOTS,)),
            sems((SLOTS,)),
            sems((SLOTS,)),
            sems((SLOTS,)),
            sems((8,)),
            sems((8,)),
            sems((2,)),
            sems((2,)),
            sems((NX,)),
            sems((NX,)),
            sems((NZ,)),
            sems((NZ,)),
            sems((NX,)),
            sems((NX,)),
            sems((NZ,)),
            sems((NZ,)),
        ],
        compiler_params=pltpu.CompilerParams(collective_id=0, has_side_effects=True),
        name="window",
    )(state, rate, cotangent, dest.reshape(1, COLUMNS), w_in[0], w_out[0])
    new_state, adjoint, grads = pl.pallas_call(
        put_out,
        out_shape=(
            jax.ShapeDtypeStruct((SIDE, SIDE, FEATS), F32),
            jax.ShapeDtypeStruct((SIDE, SIDE, FEATS), BF16),
            jax.ShapeDtypeStruct((HID // 128 * 8, 128), F32),
        ),
        in_specs=[vmem] * 3,
        out_specs=(hbm,) * 3,
        scratch_shapes=[sems((3,))],
        name="put_out",
    )(*(pltpu.with_memory_space_constraint(r, pltpu.VMEM) for r in results))
    return new_state, adjoint, grads[None]


def solution(mesh):
    in_specs = (
        P("row", ("grp", "col"), None),
        P("row", ("grp", "col")),
        P("row", ("grp", "col"), None),
        P("row", ("grp", "col"), None, None),
        P("grp", None, None),
        P("grp", None, None),
    )
    out_specs = (
        P("row", ("grp", "col"), None),
        P("row", ("grp", "col"), None),
        P("grp", ("row", "col"), None),
    )
    return jax.shard_map(local, mesh=mesh, in_specs=in_specs, out_specs=out_specs, check_vma=False)
```

```python
import jax
import jax.numpy as jnp
from jax import lax
from jax.experimental import pallas as pl
from jax.experimental.pallas import tpu as pltpu
from jax.sharding import PartitionSpec as P

F32, BF16, I32 = jnp.float32, jnp.bfloat16, jnp.int32
MESH = pl.DeviceIdType.MESH

STEPS = 4
SIDE = 16
FEATS = 256
HID = 1024
CAP = 32
ROWS, BLOCKS = 32, 32
NX, NZ = 8, 4
NY, NL = 8, 2
SLOTS = NY * NL
COLUMNS = SIDE * SIDE
WIDE = FEATS + 128
XF = 640
TN = 256

OFFSETS = sorted(
    ((dy, dl) for dy in range(NY) for dl in range(NL)),
    key=lambda o: 4 * ((4 - min(o[0], 8 - o[0])) % 4) + 2 * (o[0] >= 4) + o[1],
)
SENDING = [2, 3, 1] + list(range(4, SLOTS))
SIDES = [(0, 1), (0, -1), (1, 0), (-1, 0), (1, 1), (1, -1), (-1, 1), (-1, -1)]
FAR_X = [4, 3, 5, 2, 6, 1, 7]
FAR_Z = [2, 1, 3]
PAIR = BF16


def iota(shape, dim):
    return lax.broadcasted_iota(I32, shape, dim)


def kernel(
    state_hbm,
    rate_hbm,
    cot_hbm,
    dest_hbm,
    win_hbm,
    wout_hbm,
    new_ref,
    adj_ref,
    grad_ref,
    state_ref,
    rate_ref,
    cot_ref,
    dest_ref,
    win,
    wout,
    send,
    recv,
    back,
    home,
    places_ref,
    act_ref,
    dpre_ref,
    edge,
    halo,
    field_a,
    field_b,
    rates,
    grads,
    pair,
    half,
    x1,
    z1,
    sum_x,
    out_x,
    z2,
    sum_z,
    out_z,
    x2,
    in_sem,
    fwd_send,
    fwd_recv,
    back_send,
    back_recv,
    edge_send,
    edge_recv,
    pair_send,
    pair_recv,
    x1_send,
    x1_recv,
    z1_send,
    z1_recv,
    x2_send,
    x2_recv,
    z2_send,
    z2_recv,
):
    row, grp, col = lax.axis_index("row"), lax.axis_index("grp"), lax.axis_index("col")
    x, z = row // NZ, row % NZ
    y, l = grp // NL, grp % NL
    block = grp * 2 + col

    def at_expert(dy, dl):
        return {"row": row, "grp": ((y + dy) % NY) * NL + (l + dl) % NL, "col": col}

    def at_source(dy, dl):
        return {"row": row, "grp": ((y + NY - dy) % NY) * NL + (l + dl) % NL, "col": col}

    def at_side(di, dj):
        there = (block + dj + BLOCKS) % BLOCKS
        return {"row": (row + di + ROWS) % ROWS, "grp": there // 2, "col": there % 2}

    def at_x(dx):
        return {"row": ((x + dx) % NX) * NZ + z, "grp": grp, "col": col}

    def at_z(dz):
        return {"row": x * NZ + (z + dz) % NZ, "grp": grp, "col": col}

    partner = {"row": row, "grp": grp, "col": 1 - col}

    loads = [
        pltpu.make_async_copy(src, dst, in_sem.at[n])
        for n, (src, dst) in enumerate(
            (
                (dest_hbm, dest_ref),
                (state_hbm, state_ref),
                (cot_hbm, cot_ref),
                (rate_hbm, rate_ref),
                (win_hbm, win),
                (wout_hbm, wout),
            )
        )
    ]
    for copy in loads:
        copy.start()

    barrier = pltpu.get_barrier_semaphore()
    greeted = (
        [at_expert(*OFFSETS[t]) for t in SENDING]
        + [at_side(*o) for o in SIDES]
        + [at_x(dx) for dx in FAR_X]
        + [at_z(dz) for dz in FAR_Z]
        + [partner]
    )
    for there in greeted:
        pl.semaphore_signal(barrier, inc=1, device_id=there, device_id_type=MESH)

    def remote(src, dst, sent, came, there):
        return pltpu.make_async_remote_copy(
            src_ref=src, dst_ref=dst, send_sem=sent, recv_sem=came, device_id=there, device_id_type=MESH
        )

    loads[0].wait()

    dest = dest_ref[...]
    dy = ((dest >> 1) - y) & (NY - 1)
    dl = (dest & 1) ^ l
    slot = ((4 - jnp.minimum(dy, NY - dy)) & 3) * 4 + jnp.where(dy >= 4, 2, 0) + dl
    chosen = jnp.where(iota((SLOTS, COLUMNS), 0) == slot, 1.0, 0.0)
    upto = jnp.where(
        iota((COLUMNS, COLUMNS), 0) <= iota((COLUMNS, COLUMNS), 1), 1.0, 0.0
    ).astype(BF16)
    ranks = jnp.dot(chosen.astype(BF16), upto, preferred_element_type=F32)
    rank = jnp.sum(chosen * ranks, axis=0, keepdims=True) - 1.0
    places = slot.astype(F32) * CAP + rank
    places_ref[...] = places
    placing = jnp.where(
        iota((SLOTS * CAP, COLUMNS), 0) == places.astype(I32), 1.0, 0.0
    ).astype(BF16)
    loads[1].wait()
    cells = state_ref[...].astype(BF16)
    packed = jnp.dot(placing, cells.reshape(COLUMNS, FEATS), preferred_element_type=F32)
    packed = packed.astype(BF16).reshape(SLOTS, CAP, FEATS)
    send[:, :, 0:FEATS] = packed
    recv[0, :, 0:FEATS] = packed[0]
    loads[2].wait()
    packed = 0.5 * jnp.dot(
        placing, cot_ref[...].reshape(COLUMNS, FEATS), preferred_element_type=F32
    )
    packed = packed.astype(BF16).reshape(SLOTS, CAP, FEATS)
    send[:, :, FEATS:] = packed
    recv[0, :, FEATS:] = packed[0]

    pl.semaphore_wait(barrier, len(greeted))

    fwd = {
        t: remote(send.at[t], recv.at[t], fwd_send.at[t], fwd_recv.at[t], at_expert(*OFFSETS[t]))
        for t in SENDING
    }
    for t in SENDING[:3]:
        fwd[t].start()

    loads[3].wait()
    edge[:, :, :, 0:FEATS] = cells.reshape(SIDE, 2, 8, FEATS)
    diagonal = iota((SIDE, SIDE), 0) == iota((SIDE, SIDE), 1)
    for i in range(SIDE):
        line = jnp.broadcast_to(rate_ref[i : i + 1, :], (SIDE, SIDE))
        line = jnp.sum(jnp.where(diagonal, line, 0.0), axis=1, keepdims=True)
        line = jnp.broadcast_to(line, (SIDE, 128))
        rates[4 + i, 8 : 8 + SIDE, :] = line
        edge[i, :, :, FEATS:] = line.astype(BF16).reshape(2, 8, 128)

    span = {-1: (slice(0, 4), slice(20, 24)), 1: (slice(12, 16), slice(0, 4)), 0: (slice(0, 16), slice(4, 20))}
    tile = {-1: (slice(0, 1), slice(3, 4)), 1: (slice(1, 2), slice(0, 1)), 0: (slice(0, 2), slice(1, 3))}
    edges = [
        remote(
            edge.at[span[di][0], tile[dj][0]],
            halo.at[span[di][1], tile[dj][1]],
            edge_send.at[n],
            edge_recv.at[n],
            at_side(di, dj),
        )
        for n, (di, dj) in enumerate(SIDES)
    ]
    for copy in edges:
        copy.start()
    for t in SENDING[3:]:
        fwd[t].start()

    for copy in loads[4:]:
        copy.wait()

    homeward = {
        t: remote(back.at[t], home.at[t], back_send.at[t], back_recv.at[t], at_source(*OFFSETS[t]))
        for t in SENDING
    }
    def answer(g):
        lines = slice(128 * g, 128 * g + 128)
        across = (((1,), (1,)), ((), ()))
        tend = lax.dot_general(act_ref[lines, :], wout[...], across, preferred_element_type=F32)
        adjoint = lax.dot_general(dpre_ref[lines, :], win[...], across, preferred_element_type=F32)
        tend = tend.astype(BF16).reshape(4, CAP, FEATS)
        adjoint = adjoint.astype(BF16).reshape(4, CAP, FEATS)
        back[4 * g : 4 * g + 4, :, 0:FEATS] = tend
        back[4 * g : 4 * g + 4, :, FEATS:] = adjoint
        if g == 0:
            home[0, :, 0:FEATS] = tend[0]
            home[0, :, FEATS:] = adjoint[0]

    for g in range(4):
        for t in range(4 * g, 4 * g + 4):
            if t:
                fwd[t].wait_recv()
        if g == 3:
            for t in SENDING[:11]:
                homeward[t].start()
        lines = slice(128 * g, 128 * g + 128)
        came = recv[4 * g : 4 * g + 4].reshape(128, 2 * FEATS)
        columns, dtend = came[:, 0:FEATS], came[:, FEATS:]
        for h in range(0, HID, TN):
            pre = jnp.dot(columns, win[:, h : h + TN], preferred_element_type=F32)
            dact = jnp.dot(dtend, wout[:, h : h + TN], preferred_element_type=F32)
            sigma = 1.0 / (1.0 + jnp.exp(-pre))
            act_ref[lines, h : h + TN] = (pre * sigma).astype(BF16)
            slope = sigma * (1.0 + pre * (1.0 - sigma))
            dpre_ref[lines, h : h + TN] = (dact * slope).astype(BF16)
        if g < 3:
            answer(g)
        if g == 1:
            for copy in edges:
                copy.wait_recv()
            for top in (0, 20):
                cells = halo[top : top + 4].astype(F32).reshape(4, 32, WIDE)
                field_a[top : top + 4] = cells[:, :, 0:FEATS]
                rates[top : top + 4] = cells[:, :, FEATS:]
            for t in (0, 3):
                cells = halo[4:20, t].astype(F32)
                field_a[4:20, 8 * t : 8 * t + 8] = cells[:, :, 0:FEATS]
                rates[4:20, 8 * t : 8 * t + 8] = cells[:, :, FEATS:]
            field_a[4:20, 8:24] = state_ref[...]
            old, new = field_a, field_b
            for step in range(1, STEPS + 1):

                def advance(n, carry, old=old, new=new, step=step):
                    i = step + 2 * n
                    here = old[pl.ds(i, 2)]
                    beside = old[pl.ds(i - 1, 2)] + old[pl.ds(i + 1, 2)]
                    beside = beside + pltpu.roll(here, 1, 1) + pltpu.roll(here, 31, 1)
                    pace = rates[pl.ds(i, 2)]
                    pace = jnp.concatenate([pace, pace], axis=2)
                    new[pl.ds(i, 2)] = here + pace * (beside - 4.0 * here)
                    return carry

                lax.fori_loop(0, 12 - step, advance, 0)
                old, new = new, old

    parts = (slice(0, XF), slice(XF, HID))
    pairs = []
    for n, part in enumerate(parts):
        for first, hidden, out in ((FEATS, act_ref, slice(16, 32)), (0, dpre_ref, slice(0, 16))):
            left = recv[:, :, first : first + FEATS].reshape(SLOTS * CAP, FEATS)
            for h in range(part.start, part.stop, TN):
                width = min(TN, part.stop - h)
                piece = lax.dot_general(
                    left, hidden[:, h : h + width], (((0,), (0,)), ((), ())), preferred_element_type=F32
                )
                grads[out, :, :, h : h + width] = piece.reshape(16, 2, 8, width).astype(PAIR)
        copy = remote(
            grads.at[:, 1 - col, :, part], pair.at[:, :, part], pair_send.at[n], pair_recv.at[n], partner
        )
        copy.start()
        pairs.append(copy)
    answer(3)
    for t in SENDING[11:]:
        homeward[t].start()
    first_x = [
        remote(
            half.at[(x + dx) % NX, :, :, 0:XF], x1.at[dx], x1_send.at[dx], x1_recv.at[dx], at_x(dx)
        )
        for dx in FAR_X
    ]
    first_z = [
        remote(
            half.at[:, (z + dz) % NZ, :, XF:], z1.at[dz], z1_send.at[dz], z1_recv.at[dz], at_z(dz)
        )
        for dz in FAR_Z
    ]
    for part, copy, onward in zip(parts, pairs, (first_x, first_z)):
        copy.wait_recv()
        both = grads[:, col, :, part].astype(F32) + pair[:, :, part].astype(F32)
        half[:, :, :, part] = both.astype(BF16).reshape(NX, NZ, 8, part.stop - part.start)
        for there in onward:
            there.start()

    for copy in first_x:
        copy.wait_recv()
    total = half[x, :, :, 0:XF].astype(F32)
    for dx in range(1, NX):
        total = total + x1[dx].astype(F32)
    sum_x[...] = total
    out_x[...] = total.astype(BF16)
    last_z = [
        remote(out_x.at[(z + dz) % NZ], z2.at[dz], z2_send.at[dz], z2_recv.at[dz], at_z(dz)) for dz in FAR_Z
    ]
    for copy in last_z:
        copy.start()
    for copy in first_z:
        copy.wait_recv()
    total = half[:, z, :, XF:].astype(F32)
    for dz in range(1, NZ):
        total = total + z1[dz].astype(F32)
    sum_z[...] = total
    out_z[...] = total.astype(BF16)
    last_x = [
        remote(out_z.at[(x + dx) % NX], x2.at[dx], x2_send.at[dx], x2_recv.at[dx], at_x(dx)) for dx in FAR_X
    ]
    for copy in last_x:
        copy.start()

    for t in SENDING:
        homeward[t].wait_recv()
    square = iota((COLUMNS, COLUMNS), 0) == iota((COLUMNS, COLUMNS), 1)
    tall = jnp.where(square, jnp.broadcast_to(places_ref[...], (COLUMNS, COLUMNS)), 0.0)
    tall = jnp.sum(tall, axis=1, keepdims=True).astype(I32)
    picking = jnp.where(iota((COLUMNS, SLOTS * CAP), 1) == tall, 1.0, 0.0).astype(BF16)
    tend = jnp.dot(
        picking, home[:, :, 0:FEATS].reshape(SLOTS * CAP, FEATS), preferred_element_type=F32
    )
    new_ref[...] = old[4:20, 8:24] + 0.5 * tend.reshape(SIDE, SIDE, FEATS)
    adjoint = jnp.dot(
        picking, home[:, :, FEATS:].reshape(SLOTS * CAP, FEATS), preferred_element_type=F32
    )
    adj_ref[...] = adjoint.astype(BF16).reshape(SIDE, SIDE, FEATS)

    for copy in last_z:
        copy.wait_recv()
    total = sum_x[z]
    for dz in range(1, NZ):
        total = total + z2[dz].astype(F32)
    for h in range(0, XF, 128):
        grad_ref[pl.ds(h // 128, 8, stride=8), :] = total[:, h : h + 128]
    for copy in last_x:
        copy.wait_recv()
    total = sum_z[x]
    for dx in range(1, NX):
        total = total + x2[dx].astype(F32)
    for h in range(XF, HID, 128):
        grad_ref[pl.ds(h // 128, 8, stride=8), :] = total[:, h - XF : h - XF + 128]

    for t in SENDING:
        fwd[t].wait_send()
        homeward[t].wait_send()
    for copy in edges + pairs + first_x + first_z + last_x + last_z:
        copy.wait_send()


def put_out(*refs):
    copies = [pltpu.make_async_copy(refs[n], refs[3 + n], refs[6].at[n]) for n in range(3)]
    for copy in copies:
        copy.start()
    for copy in copies:
        copy.wait()


def local(state, rate, cotangent, dest, w_in, w_out):
    vmem = pl.BlockSpec(memory_space=pltpu.VMEM)
    hbm = pl.BlockSpec(memory_space=pl.ANY)
    sems = pltpu.SemaphoreType.DMA
    results = pl.pallas_call(
        kernel,
        out_shape=(
            pltpu.VMEM((SIDE, SIDE, FEATS), F32),
            pltpu.VMEM((SIDE, SIDE, FEATS), BF16),
            pltpu.VMEM((HID // 128 * 8, 128), F32),
        ),
        in_specs=[hbm] * 6,
        out_specs=(vmem, vmem, vmem),
        scratch_shapes=[
            pltpu.VMEM((SIDE, SIDE, FEATS), F32),
            pltpu.VMEM((SIDE, SIDE), F32),
            pltpu.VMEM((SIDE, SIDE, FEATS), BF16),
            pltpu.VMEM((1, COLUMNS), I32),
            pltpu.VMEM((FEATS, HID), BF16),
            pltpu.VMEM((FEATS, HID), BF16),
            pltpu.VMEM((SLOTS, CAP, 2 * FEATS), BF16),
            pltpu.VMEM((SLOTS, CAP, 2 * FEATS), BF16),
            pltpu.VMEM((SLOTS, CAP, 2 * FEATS), BF16),
            pltpu.VMEM((SLOTS, CAP, 2 * FEATS), BF16),
            pltpu.VMEM((1, COLUMNS), F32),
            pltpu.VMEM((SLOTS * CAP, HID), BF16),
            pltpu.VMEM((SLOTS * CAP, HID), BF16),
            pltpu.VMEM((SIDE, 2, 8, WIDE), BF16),
            pltpu.VMEM((24, 4, 8, WIDE), BF16),
            pltpu.VMEM((24, 32, FEATS), F32),
            pltpu.VMEM((24, 32, FEATS), F32),
            pltpu.VMEM((24, 32, 128), F32),
            pltpu.VMEM((32, 2, 8, HID), PAIR),
            pltpu.VMEM((32, 8, HID), PAIR),
            pltpu.VMEM((NX, NZ, 8, HID), BF16),
            pltpu.VMEM((NX, NZ, 8, XF), BF16),
            pltpu.VMEM((NZ, NX, 8, HID - XF), BF16),
            pltpu.VMEM((NZ, 8, XF), F32),
            pltpu.VMEM((NZ, 8, XF), BF16),
            pltpu.VMEM((NZ, 8, XF), BF16),
            pltpu.VMEM((NX, 8, HID - XF), F32),
            pltpu.VMEM((NX, 8, HID - XF), BF16),
            pltpu.VMEM((NX, 8, HID - XF), BF16),
            sems((6,)),
            sems((SLOTS,)),
            sems((SLOTS,)),
            sems((SLOTS,)),
            sems((SLOTS,)),
            sems((8,)),
            sems((8,)),
            sems((2,)),
            sems((2,)),
            sems((NX,)),
            sems((NX,)),
            sems((NZ,)),
            sems((NZ,)),
            sems((NX,)),
            sems((NX,)),
            sems((NZ,)),
            sems((NZ,)),
        ],
        compiler_params=pltpu.CompilerParams(collective_id=0, has_side_effects=True),
        name="window",
    )(state, rate, cotangent, dest.reshape(1, COLUMNS), w_in[0], w_out[0])
    new_state, adjoint, grads = pl.pallas_call(
        put_out,
        out_shape=(
            jax.ShapeDtypeStruct((SIDE, SIDE, FEATS), F32),
            jax.ShapeDtypeStruct((SIDE, SIDE, FEATS), BF16),
            jax.ShapeDtypeStruct((HID // 128 * 8, 128), F32),
        ),
        in_specs=[vmem] * 3,
        out_specs=(hbm,) * 3,
        scratch_shapes=[sems((3,))],
        name="put_out",
    )(*(pltpu.with_memory_space_constraint(r, pltpu.VMEM) for r in results))
    return new_state, adjoint, grads[None]


def solution(mesh):
    in_specs = (
        P("row", ("grp", "col"), None),
        P("row", ("grp", "col")),
        P("row", ("grp", "col"), None),
        P("row", ("grp", "col"), None, None),
        P("grp", None, None),
        P("grp", None, None),
    )
    out_specs = (
        P("row", ("grp", "col"), None),
        P("row", ("grp", "col"), None),
        P("grp", ("row", "col"), None),
    )
    return jax.shard_map(local, mesh=mesh, in_specs=in_specs, out_specs=out_specs, check_vma=False)
```

```python
import jax
import jax.numpy as jnp
from jax import lax
from jax.experimental import pallas as pl
from jax.experimental.pallas import tpu as pltpu
from jax.sharding import PartitionSpec as P

F32, BF16, I32 = jnp.float32, jnp.bfloat16, jnp.int32
MESH = pl.DeviceIdType.MESH

STEPS = 4
SIDE = 16
FEATS = 256
HID = 1024
CAP = 32
ROWS, BLOCKS = 32, 32
NX, NZ = 8, 4
NY, NL = 8, 2
SLOTS = NY * NL
COLUMNS = SIDE * SIDE
XF = 640
TN = 256

OFFSETS = sorted(
    ((dy, dl) for dy in range(NY) for dl in range(NL)),
    key=lambda o: 4 * ((4 - min(o[0], 8 - o[0])) % 4) + 2 * (o[0] >= 4) + o[1],
)
SENDING = [2, 3, 1] + list(range(4, SLOTS))
SIDES = [(0, 1), (0, -1), (1, 0), (-1, 0), (1, 1), (1, -1), (-1, 1), (-1, -1)]
FAR_X = [4, 3, 5, 2, 6, 1, 7]
FAR_Z = [2, 1, 3]
PAIR = BF16


def iota(shape, dim):
    return lax.broadcasted_iota(I32, shape, dim)


def kernel(
    state_hbm,
    rate_hbm,
    cot_hbm,
    dest_hbm,
    win_hbm,
    wout_hbm,
    new_ref,
    adj_ref,
    grad_ref,
    state_ref,
    rate_ref,
    cot_ref,
    dest_ref,
    win,
    wout,
    send,
    recv,
    back,
    home,
    places_ref,
    act_ref,
    dpre_ref,
    edge,
    halo,
    pace_out,
    pace_in,
    field_a,
    field_b,
    rates,
    grads,
    pair,
    half,
    x1,
    z1,
    sum_x,
    out_x,
    z2,
    sum_z,
    out_z,
    x2,
    in_sem,
    fwd_send,
    fwd_recv,
    back_send,
    back_recv,
    edge_send,
    edge_recv,
    pace_send,
    pace_recv,
    pair_send,
    pair_recv,
    x1_send,
    x1_recv,
    z1_send,
    z1_recv,
    x2_send,
    x2_recv,
    z2_send,
    z2_recv,
):
    row, grp, col = lax.axis_index("row"), lax.axis_index("grp"), lax.axis_index("col")
    x, z = row // NZ, row % NZ
    y, l = grp // NL, grp % NL
    block = grp * 2 + col

    def at_expert(dy, dl):
        return {"row": row, "grp": ((y + dy) % NY) * NL + (l + dl) % NL, "col": col}

    def at_source(dy, dl):
        return {"row": row, "grp": ((y + NY - dy) % NY) * NL + (l + dl) % NL, "col": col}

    def at_side(di, dj):
        there = (block + dj + BLOCKS) % BLOCKS
        return {"row": (row + di + ROWS) % ROWS, "grp": there // 2, "col": there % 2}

    def at_x(dx):
        return {"row": ((x + dx) % NX) * NZ + z, "grp": grp, "col": col}

    def at_z(dz):
        return {"row": x * NZ + (z + dz) % NZ, "grp": grp, "col": col}

    partner = {"row": row, "grp": grp, "col": 1 - col}

    loads = [
        pltpu.make_async_copy(src, dst, in_sem.at[n])
        for n, (src, dst) in enumerate(
            (
                (dest_hbm, dest_ref),
                (state_hbm, state_ref),
                (cot_hbm, cot_ref),
                (rate_hbm, rate_ref),
                (win_hbm, win),
                (wout_hbm, wout),
            )
        )
    ]
    for copy in loads:
        copy.start()

    barrier = pltpu.get_barrier_semaphore()
    greeted = (
        [at_expert(*OFFSETS[t]) for t in SENDING]
        + [at_side(*o) for o in SIDES]
        + [at_x(dx) for dx in FAR_X]
        + [at_z(dz) for dz in FAR_Z]
        + [partner]
    )
    for there in greeted:
        pl.semaphore_signal(barrier, inc=1, device_id=there, device_id_type=MESH)

    def remote(src, dst, sent, came, there):
        return pltpu.make_async_remote_copy(
            src_ref=src, dst_ref=dst, send_sem=sent, recv_sem=came, device_id=there, device_id_type=MESH
        )

    loads[0].wait()

    dest = dest_ref[...]
    dy = ((dest >> 1) - y) & (NY - 1)
    dl = (dest & 1) ^ l
    slot = ((4 - jnp.minimum(dy, NY - dy)) & 3) * 4 + jnp.where(dy >= 4, 2, 0) + dl
    chosen = jnp.where(iota((SLOTS, COLUMNS), 0) == slot, 1.0, 0.0)
    upto = jnp.where(
        iota((COLUMNS, COLUMNS), 0) <= iota((COLUMNS, COLUMNS), 1), 1.0, 0.0
    ).astype(BF16)
    ranks = jnp.dot(chosen.astype(BF16), upto, preferred_element_type=F32)
    rank = jnp.sum(chosen * ranks, axis=0, keepdims=True) - 1.0
    places = slot.astype(F32) * CAP + rank
    places_ref[...] = places
    placing = jnp.where(
        iota((SLOTS * CAP, COLUMNS), 0) == places.astype(I32), 1.0, 0.0
    ).astype(BF16)
    loads[1].wait()
    cells = state_ref[...].astype(BF16)
    packed = jnp.dot(placing, cells.reshape(COLUMNS, FEATS), preferred_element_type=F32)
    packed = packed.astype(BF16).reshape(SLOTS, CAP, FEATS)
    send[:, :, 0:FEATS] = packed
    recv[0, :, 0:FEATS] = packed[0]
    loads[2].wait()
    packed = 0.5 * jnp.dot(
        placing, cot_ref[...].reshape(COLUMNS, FEATS), preferred_element_type=F32
    )
    packed = packed.astype(BF16).reshape(SLOTS, CAP, FEATS)
    send[:, :, FEATS:] = packed
    recv[0, :, FEATS:] = packed[0]

    pl.semaphore_wait(barrier, len(greeted))

    fwd = {
        t: remote(send.at[t], recv.at[t], fwd_send.at[t], fwd_recv.at[t], at_expert(*OFFSETS[t]))
        for t in SENDING
    }
    for t in SENDING[:3]:
        fwd[t].start()

    loads[3].wait()
    edge[...] = cells.reshape(SIDE, 2, 8, FEATS)
    pace_out[...] = jnp.zeros_like(pace_out)
    pace_out[:, 0:SIDE] = rate_ref[...]

    span = {-1: (slice(0, 4), slice(20, 24)), 1: (slice(12, 16), slice(0, 4)), 0: (slice(0, 16), slice(4, 20))}
    tile = {-1: (slice(0, 1), slice(3, 4)), 1: (slice(1, 2), slice(0, 1)), 0: (slice(0, 2), slice(1, 3))}
    edges = [
        remote(
            edge.at[span[di][0], tile[dj][0]],
            halo.at[span[di][1], tile[dj][1]],
            edge_send.at[n],
            edge_recv.at[n],
            at_side(di, dj),
        )
        for n, (di, dj) in enumerate(SIDES)
    ]
    paces = [
        remote(pace_out, pace_in.at[n], pace_send.at[n], pace_recv.at[n], at_side(*o))
        for n, o in enumerate(SIDES)
    ]
    for t in SENDING[3:]:
        fwd[t].start()
    for copy in edges + paces:
        copy.start()

    for copy in loads[4:]:
        copy.wait()

    homeward = {
        t: remote(back.at[t], home.at[t], back_send.at[t], back_recv.at[t], at_source(*OFFSETS[t]))
        for t in SENDING
    }
    def spread(line, first, i, j, width):
        own = iota((width, 128), 1) == iota((width, 128), 0) + first
        line = jnp.where(own, jnp.broadcast_to(line, (width, 128)), 0.0)
        line = jnp.sum(line, axis=1, keepdims=True)
        rates[i, j : j + width, :] = jnp.broadcast_to(line, (width, 128))

    def answer(g):
        lines = slice(128 * g, 128 * g + 128)
        across = (((1,), (1,)), ((), ()))
        tend = lax.dot_general(act_ref[lines, :], wout[...], across, preferred_element_type=F32)
        adjoint = lax.dot_general(dpre_ref[lines, :], win[...], across, preferred_element_type=F32)
        tend = tend.astype(BF16).reshape(4, CAP, FEATS)
        adjoint = adjoint.astype(BF16).reshape(4, CAP, FEATS)
        back[4 * g : 4 * g + 4, :, 0:FEATS] = tend
        back[4 * g : 4 * g + 4, :, FEATS:] = adjoint
        if g == 0:
            home[0, :, 0:FEATS] = tend[0]
            home[0, :, FEATS:] = adjoint[0]

    for g in range(4):
        for t in range(4 * g, 4 * g + 4):
            if t:
                fwd[t].wait_recv()
        if g == 3:
            for t in SENDING[:11]:
                homeward[t].start()
        lines = slice(128 * g, 128 * g + 128)
        came = recv[4 * g : 4 * g + 4].reshape(128, 2 * FEATS)
        columns, dtend = came[:, 0:FEATS], came[:, FEATS:]
        for h in range(0, HID, TN):
            pre = jnp.dot(columns, win[:, h : h + TN], preferred_element_type=F32)
            dact = jnp.dot(dtend, wout[:, h : h + TN], preferred_element_type=F32)
            sigma = 1.0 / (1.0 + jnp.exp(-pre))
            act_ref[lines, h : h + TN] = (pre * sigma).astype(BF16)
            slope = sigma * (1.0 + pre * (1.0 - sigma))
            dpre_ref[lines, h : h + TN] = (dact * slope).astype(BF16)
        if g < 3:
            answer(g)

    parts = (slice(0, XF), slice(XF, HID))
    pairs = []
    for n, part in enumerate(parts):
        for first, hidden, out in ((FEATS, act_ref, slice(16, 32)), (0, dpre_ref, slice(0, 16))):
            left = recv[:, :, first : first + FEATS].reshape(SLOTS * CAP, FEATS)
            for h in range(part.start, part.stop, TN):
                width = min(TN, part.stop - h)
                piece = lax.dot_general(
                    left, hidden[:, h : h + width], (((0,), (0,)), ((), ())), preferred_element_type=F32
                )
                grads[out, :, :, h : h + width] = piece.reshape(16, 2, 8, width).astype(PAIR)
        copy = remote(
            grads.at[:, 1 - col, :, part], pair.at[:, :, part], pair_send.at[n], pair_recv.at[n], partner
        )
        copy.start()
        pairs.append(copy)
    answer(3)
    for t in SENDING[11:]:
        homeward[t].start()
    first_x = [
        remote(
            half.at[(x + dx) % NX, :, :, 0:XF], x1.at[dx], x1_send.at[dx], x1_recv.at[dx], at_x(dx)
        )
        for dx in FAR_X
    ]
    first_z = [
        remote(
            half.at[:, (z + dz) % NZ, :, XF:], z1.at[dz], z1_send.at[dz], z1_recv.at[dz], at_z(dz)
        )
        for dz in FAR_Z
    ]
    for part, copy, onward in zip(parts, pairs, (first_x, first_z)):
        copy.wait_recv()
        both = grads[:, col, :, part].astype(F32) + pair[:, :, part].astype(F32)
        half[:, :, :, part] = both.astype(BF16).reshape(NX, NZ, 8, part.stop - part.start)
        for there in onward:
            there.start()

    for i in range(SIDE):
        spread(pace_out[i : i + 1, :], 0, 4 + i, 8, SIDE)
    for copy in edges + paces:
        copy.wait_recv()
    for n, (di, dj) in enumerate(SIDES):
        (source, target), (left, right) = span[di], tile[dj]
        for i in range(target.stop - target.start):
            spread(
                pace_in[n, source.start + i : source.start + i + 1, :],
                8 * left.start,
                target.start + i,
                8 * right.start,
                8 * (right.stop - right.start),
            )
    for top in (0, 20):
        field_a[top : top + 4] = halo[top : top + 4].astype(F32).reshape(4, 32, FEATS)
    for t in (0, 3):
        field_a[4:20, 8 * t : 8 * t + 8] = halo[4:20, t].astype(F32)
    field_a[4:20, 8:24] = state_ref[...]
    old, new = field_a, field_b
    for step in range(1, STEPS + 1):

        def advance(n, carry, old=old, new=new, step=step):
            i = step + 2 * n
            here = old[pl.ds(i, 2)]
            beside = old[pl.ds(i - 1, 2)] + old[pl.ds(i + 1, 2)]
            beside = beside + pltpu.roll(here, 1, 1) + pltpu.roll(here, 31, 1)
            pace = rates[pl.ds(i, 2)]
            pace = jnp.concatenate([pace, pace], axis=2)
            new[pl.ds(i, 2)] = here + pace * (beside - 4.0 * here)
            return carry

        lax.fori_loop(0, 12 - step, advance, 0)
        old, new = new, old

    for copy in first_x:
        copy.wait_recv()
    total = half[x, :, :, 0:XF].astype(F32)
    for dx in range(1, NX):
        total = total + x1[dx].astype(F32)
    sum_x[...] = total
    out_x[...] = total.astype(BF16)
    last_z = [
        remote(out_x.at[(z + dz) % NZ], z2.at[dz], z2_send.at[dz], z2_recv.at[dz], at_z(dz)) for dz in FAR_Z
    ]
    for copy in last_z:
        copy.start()
    for copy in first_z:
        copy.wait_recv()
    total = half[:, z, :, XF:].astype(F32)
    for dz in range(1, NZ):
        total = total + z1[dz].astype(F32)
    sum_z[...] = total
    out_z[...] = total.astype(BF16)
    last_x = [
        remote(out_z.at[(x + dx) % NX], x2.at[dx], x2_send.at[dx], x2_recv.at[dx], at_x(dx)) for dx in FAR_X
    ]
    for copy in last_x:
        copy.start()

    for t in SENDING:
        homeward[t].wait_recv()
    square = iota((COLUMNS, COLUMNS), 0) == iota((COLUMNS, COLUMNS), 1)
    tall = jnp.where(square, jnp.broadcast_to(places_ref[...], (COLUMNS, COLUMNS)), 0.0)
    tall = jnp.sum(tall, axis=1, keepdims=True).astype(I32)
    picking = jnp.where(iota((COLUMNS, SLOTS * CAP), 1) == tall, 1.0, 0.0).astype(BF16)
    tend = jnp.dot(
        picking, home[:, :, 0:FEATS].reshape(SLOTS * CAP, FEATS), preferred_element_type=F32
    )
    new_ref[...] = old[4:20, 8:24] + 0.5 * tend.reshape(SIDE, SIDE, FEATS)
    adjoint = jnp.dot(
        picking, home[:, :, FEATS:].reshape(SLOTS * CAP, FEATS), preferred_element_type=F32
    )
    adj_ref[...] = adjoint.astype(BF16).reshape(SIDE, SIDE, FEATS)

    for copy in last_z:
        copy.wait_recv()
    total = sum_x[z]
    for dz in range(1, NZ):
        total = total + z2[dz].astype(F32)
    for h in range(0, XF, 128):
        grad_ref[pl.ds(h // 128, 8, stride=8), :] = total[:, h : h + 128]
    for copy in last_x:
        copy.wait_recv()
    total = sum_z[x]
    for dx in range(1, NX):
        total = total + x2[dx].astype(F32)
    for h in range(XF, HID, 128):
        grad_ref[pl.ds(h // 128, 8, stride=8), :] = total[:, h - XF : h - XF + 128]

    for t in SENDING:
        fwd[t].wait_send()
        homeward[t].wait_send()
    for copy in edges + paces + pairs + first_x + first_z + last_x + last_z:
        copy.wait_send()


def put_out(*refs):
    copies = [pltpu.make_async_copy(refs[n], refs[3 + n], refs[6].at[n]) for n in range(3)]
    for copy in copies:
        copy.start()
    for copy in copies:
        copy.wait()


def local(state, rate, cotangent, dest, w_in, w_out):
    vmem = pl.BlockSpec(memory_space=pltpu.VMEM)
    hbm = pl.BlockSpec(memory_space=pl.ANY)
    sems = pltpu.SemaphoreType.DMA
    results = pl.pallas_call(
        kernel,
        out_shape=(
            pltpu.VMEM((SIDE, SIDE, FEATS), F32),
            pltpu.VMEM((SIDE, SIDE, FEATS), BF16),
            pltpu.VMEM((HID // 128 * 8, 128), F32),
        ),
        in_specs=[hbm] * 6,
        out_specs=(vmem, vmem, vmem),
        scratch_shapes=[
            pltpu.VMEM((SIDE, SIDE, FEATS), F32),
            pltpu.VMEM((SIDE, SIDE), F32),
            pltpu.VMEM((SIDE, SIDE, FEATS), BF16),
            pltpu.VMEM((1, COLUMNS), I32),
            pltpu.VMEM((FEATS, HID), BF16),
            pltpu.VMEM((FEATS, HID), BF16),
            pltpu.VMEM((SLOTS, CAP, 2 * FEATS), BF16),
            pltpu.VMEM((SLOTS, CAP, 2 * FEATS), BF16),
            pltpu.VMEM((SLOTS, CAP, 2 * FEATS), BF16),
            pltpu.VMEM((SLOTS, CAP, 2 * FEATS), BF16),
            pltpu.VMEM((1, COLUMNS), F32),
            pltpu.VMEM((SLOTS * CAP, HID), BF16),
            pltpu.VMEM((SLOTS * CAP, HID), BF16),
            pltpu.VMEM((SIDE, 2, 8, FEATS), BF16),
            pltpu.VMEM((24, 4, 8, FEATS), BF16),
            pltpu.VMEM((SIDE, 128), F32),
            pltpu.VMEM((8, SIDE, 128), F32),
            pltpu.VMEM((24, 32, FEATS), F32),
            pltpu.VMEM((24, 32, FEATS), F32),
            pltpu.VMEM((24, 32, 128), F32),
            pltpu.VMEM((32, 2, 8, HID), PAIR),
            pltpu.VMEM((32, 8, HID), PAIR),
            pltpu.VMEM((NX, NZ, 8, HID), BF16),
            pltpu.VMEM((NX, NZ, 8, XF), BF16),
            pltpu.VMEM((NZ, NX, 8, HID - XF), BF16),
            pltpu.VMEM((NZ, 8, XF), F32),
            pltpu.VMEM((NZ, 8, XF), BF16),
            pltpu.VMEM((NZ, 8, XF), BF16),
            pltpu.VMEM((NX, 8, HID - XF), F32),
            pltpu.VMEM((NX, 8, HID - XF), BF16),
            pltpu.VMEM((NX, 8, HID - XF), BF16),
            sems((6,)),
            sems((SLOTS,)),
            sems((SLOTS,)),
            sems((SLOTS,)),
            sems((SLOTS,)),
            sems((8,)),
            sems((8,)),
            sems((8,)),
            sems((8,)),
            sems((2,)),
            sems((2,)),
            sems((NX,)),
            sems((NX,)),
            sems((NZ,)),
            sems((NZ,)),
            sems((NX,)),
            sems((NX,)),
            sems((NZ,)),
            sems((NZ,)),
        ],
        compiler_params=pltpu.CompilerParams(collective_id=0, has_side_effects=True),
        name="window",
    )(state, rate, cotangent, dest.reshape(1, COLUMNS), w_in[0], w_out[0])
    new_state, adjoint, grads = pl.pallas_call(
        put_out,
        out_shape=(
            jax.ShapeDtypeStruct((SIDE, SIDE, FEATS), F32),
            jax.ShapeDtypeStruct((SIDE, SIDE, FEATS), BF16),
            jax.ShapeDtypeStruct((HID // 128 * 8, 128), F32),
        ),
        in_specs=[vmem] * 3,
        out_specs=(hbm,) * 3,
        scratch_shapes=[sems((3,))],
        name="put_out",
    )(*(pltpu.with_memory_space_constraint(r, pltpu.VMEM) for r in results))
    return new_state, adjoint, grads[None]


def solution(mesh):
    in_specs = (
        P("row", ("grp", "col"), None),
        P("row", ("grp", "col")),
        P("row", ("grp", "col"), None),
        P("row", ("grp", "col"), None, None),
        P("grp", None, None),
        P("grp", None, None),
    )
    out_specs = (
        P("row", ("grp", "col"), None),
        P("row", ("grp", "col"), None),
        P("grp", ("row", "col"), None),
    )
    return jax.shard_map(local, mesh=mesh, in_specs=in_specs, out_specs=out_specs, check_vma=False)
```

```python
import jax
import jax.numpy as jnp
from jax import lax
from jax.experimental import pallas as pl
from jax.experimental.pallas import tpu as pltpu
from jax.sharding import PartitionSpec as P

F32, BF16, I32 = jnp.float32, jnp.bfloat16, jnp.int32
MESH = pl.DeviceIdType.MESH

STEPS = 4
SIDE = 16
FEATS = 256
HID = 1024
CAP = 32
ROWS, BLOCKS = 32, 32
NX, NZ = 8, 4
NY, NL = 8, 2
SLOTS = NY * NL
COLUMNS = SIDE * SIDE
XF = 640
TN = 256

OFFSETS = sorted(
    ((dy, dl) for dy in range(NY) for dl in range(NL)),
    key=lambda o: 4 * ((4 - min(o[0], 8 - o[0])) % 4) + 2 * (o[0] >= 4) + o[1],
)
SENDING = [2, 3, 1] + list(range(4, SLOTS))
SIDES = [(0, 1), (0, -1), (1, 0), (-1, 0), (1, 1), (1, -1), (-1, 1), (-1, -1)]
FAR_X = [4, 3, 5, 2, 6, 1, 7]
FAR_Z = [2, 1, 3]
PAIR = BF16


def iota(shape, dim):
    return lax.broadcasted_iota(I32, shape, dim)


def kernel(
    state_hbm,
    rate_hbm,
    cot_hbm,
    dest_hbm,
    win_hbm,
    wout_hbm,
    new_ref,
    adj_ref,
    grad_ref,
    state_ref,
    rate_ref,
    cot_ref,
    dest_ref,
    win,
    wout,
    send,
    recv,
    back,
    home,
    places_ref,
    act_ref,
    dpre_ref,
    edge,
    halo,
    pace_out,
    pace_in,
    field_a,
    field_b,
    rates,
    grads,
    pair,
    half,
    x1,
    z1,
    sum_x,
    out_x,
    z2,
    sum_z,
    out_z,
    x2,
    in_sem,
    fwd_send,
    fwd_recv,
    back_send,
    back_recv,
    edge_send,
    edge_recv,
    pace_send,
    pace_recv,
    pair_send,
    pair_recv,
    x1_send,
    x1_recv,
    z1_send,
    z1_recv,
    x2_send,
    x2_recv,
    z2_send,
    z2_recv,
):
    row, grp, col = lax.axis_index("row"), lax.axis_index("grp"), lax.axis_index("col")
    x, z = row // NZ, row % NZ
    y, l = grp // NL, grp % NL
    block = grp * 2 + col

    def at_expert(dy, dl):
        return {"row": row, "grp": ((y + dy) % NY) * NL + (l + dl) % NL, "col": col}

    def at_source(dy, dl):
        return {"row": row, "grp": ((y + NY - dy) % NY) * NL + (l + dl) % NL, "col": col}

    def at_side(di, dj):
        there = (block + dj + BLOCKS) % BLOCKS
        return {"row": (row + di + ROWS) % ROWS, "grp": there // 2, "col": there % 2}

    def at_x(dx):
        return {"row": ((x + dx) % NX) * NZ + z, "grp": grp, "col": col}

    def at_z(dz):
        return {"row": x * NZ + (z + dz) % NZ, "grp": grp, "col": col}

    partner = {"row": row, "grp": grp, "col": 1 - col}

    loads = [
        pltpu.make_async_copy(src, dst, in_sem.at[n])
        for n, (src, dst) in enumerate(
            (
                (dest_hbm, dest_ref),
                (state_hbm, state_ref),
                (cot_hbm, cot_ref),
                (rate_hbm, rate_ref),
                (win_hbm, win),
                (wout_hbm, wout),
            )
        )
    ]
    for copy in loads:
        copy.start()

    barrier = pltpu.get_barrier_semaphore()
    greeted = (
        [at_expert(*OFFSETS[t]) for t in SENDING]
        + [at_side(*o) for o in SIDES]
        + [at_x(dx) for dx in FAR_X]
        + [at_z(dz) for dz in FAR_Z]
        + [partner]
    )
    for there in greeted:
        pl.semaphore_signal(barrier, inc=1, device_id=there, device_id_type=MESH)

    def remote(src, dst, sent, came, there):
        return pltpu.make_async_remote_copy(
            src_ref=src, dst_ref=dst, send_sem=sent, recv_sem=came, device_id=there, device_id_type=MESH
        )

    loads[0].wait()

    dest = dest_ref[...]
    dy = ((dest >> 1) - y) & (NY - 1)
    dl = (dest & 1) ^ l
    slot = ((4 - jnp.minimum(dy, NY - dy)) & 3) * 4 + jnp.where(dy >= 4, 2, 0) + dl
    chosen = jnp.where(iota((SLOTS, COLUMNS), 0) == slot, 1.0, 0.0)
    upto = jnp.where(
        iota((COLUMNS, COLUMNS), 0) <= iota((COLUMNS, COLUMNS), 1), 1.0, 0.0
    ).astype(BF16)
    ranks = jnp.dot(chosen.astype(BF16), upto, preferred_element_type=F32)
    rank = jnp.sum(chosen * ranks, axis=0, keepdims=True) - 1.0
    places = slot.astype(F32) * CAP + rank
    places_ref[...] = places
    placing = jnp.where(
        iota((SLOTS * CAP, COLUMNS), 0) == places.astype(I32), 1.0, 0.0
    ).astype(BF16)
    loads[1].wait()
    cells = state_ref[...].astype(BF16)
    packed = jnp.dot(placing, cells.reshape(COLUMNS, FEATS), preferred_element_type=F32)
    packed = packed.astype(BF16).reshape(SLOTS, CAP, FEATS)
    send[:, :, 0:FEATS] = packed
    recv[0, :, 0:FEATS] = packed[0]
    loads[2].wait()
    packed = 0.5 * jnp.dot(
        placing, cot_ref[...].reshape(COLUMNS, FEATS), preferred_element_type=F32
    )
    packed = packed.astype(BF16).reshape(SLOTS, CAP, FEATS)
    send[:, :, FEATS:] = packed
    recv[0, :, FEATS:] = packed[0]

    pl.semaphore_wait(barrier, len(greeted))

    fwd = {
        t: remote(send.at[t], recv.at[t], fwd_send.at[t], fwd_recv.at[t], at_expert(*OFFSETS[t]))
        for t in SENDING
    }
    for t in SENDING:
        fwd[t].start()

    loads[3].wait()
    edge[...] = cells.reshape(SIDE, 2, 8, FEATS)
    pace_out[...] = jnp.zeros_like(pace_out)
    pace_out[:, 0:SIDE] = rate_ref[...]

    span = {-1: (slice(0, 4), slice(20, 24)), 1: (slice(12, 16), slice(0, 4)), 0: (slice(0, 16), slice(4, 20))}
    tile = {-1: (slice(0, 1), slice(3, 4)), 1: (slice(1, 2), slice(0, 1)), 0: (slice(0, 2), slice(1, 3))}
    edges = [
        remote(
            edge.at[span[di][0], tile[dj][0]],
            halo.at[span[di][1], tile[dj][1]],
            edge_send.at[n],
            edge_recv.at[n],
            at_side(di, dj),
        )
        for n, (di, dj) in enumerate(SIDES)
    ]
    paces = [
        remote(pace_out, pace_in.at[n], pace_send.at[n], pace_recv.at[n], at_side(*o))
        for n, o in enumerate(SIDES)
    ]
    for copy in edges + paces:
        copy.start()

    for copy in loads[4:]:
        copy.wait()

    homeward = {
        t: remote(back.at[t], home.at[t], back_send.at[t], back_recv.at[t], at_source(*OFFSETS[t]))
        for t in SENDING
    }
    def spread(line, first, i, j, width):
        own = iota((width, 128), 1) == iota((width, 128), 0) + first
        line = jnp.where(own, jnp.broadcast_to(line, (width, 128)), 0.0)
        line = jnp.sum(line, axis=1, keepdims=True)
        rates[i, j : j + width, :] = jnp.broadcast_to(line, (width, 128))

    def answer(g):
        lines = slice(128 * g, 128 * g + 128)
        across = (((1,), (1,)), ((), ()))
        tend = lax.dot_general(act_ref[lines, :], wout[...], across, preferred_element_type=F32)
        adjoint = lax.dot_general(dpre_ref[lines, :], win[...], across, preferred_element_type=F32)
        tend = tend.astype(BF16).reshape(4, CAP, FEATS)
        adjoint = adjoint.astype(BF16).reshape(4, CAP, FEATS)
        back[4 * g : 4 * g + 4, :, 0:FEATS] = tend
        back[4 * g : 4 * g + 4, :, FEATS:] = adjoint
        if g == 0:
            home[0, :, 0:FEATS] = tend[0]
            home[0, :, FEATS:] = adjoint[0]

    for g in range(4):
        for t in range(4 * g, 4 * g + 4):
            if t:
                fwd[t].wait_recv()
        if g == 3:
            for t in SENDING[:11]:
                homeward[t].start()
        lines = slice(128 * g, 128 * g + 128)
        came = recv[4 * g : 4 * g + 4].reshape(128, 2 * FEATS)
        columns, dtend = came[:, 0:FEATS], came[:, FEATS:]
        for h in range(0, HID, TN):
            pre = jnp.dot(columns, win[:, h : h + TN], preferred_element_type=F32)
            dact = jnp.dot(dtend, wout[:, h : h + TN], preferred_element_type=F32)
            sigma = 1.0 / (1.0 + jnp.exp(-pre))
            act_ref[lines, h : h + TN] = (pre * sigma).astype(BF16)
            slope = sigma * (1.0 + pre * (1.0 - sigma))
            dpre_ref[lines, h : h + TN] = (dact * slope).astype(BF16)
        if g < 3:
            answer(g)

    parts = (slice(0, XF), slice(XF, HID))
    pairs = []
    for n, part in enumerate(parts):
        for first, hidden, out in ((FEATS, act_ref, slice(16, 32)), (0, dpre_ref, slice(0, 16))):
            left = recv[:, :, first : first + FEATS].reshape(SLOTS * CAP, FEATS)
            for h in range(part.start, part.stop, TN):
                width = min(TN, part.stop - h)
                piece = lax.dot_general(
                    left, hidden[:, h : h + width], (((0,), (0,)), ((), ())), preferred_element_type=F32
                )
                grads[out, :, :, h : h + width] = piece.reshape(16, 2, 8, width).astype(PAIR)
        copy = remote(
            grads.at[:, 1 - col, :, part], pair.at[:, :, part], pair_send.at[n], pair_recv.at[n], partner
        )
        copy.start()
        pairs.append(copy)
    answer(3)
    for t in SENDING[11:]:
        homeward[t].start()
    first_x = [
        remote(
            half.at[(x + dx) % NX, :, :, 0:XF], x1.at[dx], x1_send.at[dx], x1_recv.at[dx], at_x(dx)
        )
        for dx in FAR_X
    ]
    first_z = [
        remote(
            half.at[:, (z + dz) % NZ, :, XF:], z1.at[dz], z1_send.at[dz], z1_recv.at[dz], at_z(dz)
        )
        for dz in FAR_Z
    ]
    for part, copy, onward in zip(parts, pairs, (first_x, first_z)):
        copy.wait_recv()
        both = grads[:, col, :, part].astype(F32) + pair[:, :, part].astype(F32)
        half[:, :, :, part] = both.astype(BF16).reshape(NX, NZ, 8, part.stop - part.start)
        for there in onward:
            there.start()

    for i in range(SIDE):
        spread(pace_out[i : i + 1, :], 0, 4 + i, 8, SIDE)
    for copy in edges + paces:
        copy.wait_recv()
    for n, (di, dj) in enumerate(SIDES):
        (source, target), (left, right) = span[di], tile[dj]
        for i in range(target.stop - target.start):
            spread(
                pace_in[n, source.start + i : source.start + i + 1, :],
                8 * left.start,
                target.start + i,
                8 * right.start,
                8 * (right.stop - right.start),
            )
    for top in (0, 20):
        field_a[top : top + 4] = halo[top : top + 4].astype(F32).reshape(4, 32, FEATS)
    for t in (0, 3):
        field_a[4:20, 8 * t : 8 * t + 8] = halo[4:20, t].astype(F32)
    field_a[4:20, 8:24] = state_ref[...]
    old, new = field_a, field_b
    for step in range(1, STEPS + 1):

        def advance(n, carry, old=old, new=new, step=step):
            i = step + 2 * n
            here = old[pl.ds(i, 2)]
            beside = old[pl.ds(i - 1, 2)] + old[pl.ds(i + 1, 2)]
            beside = beside + pltpu.roll(here, 1, 1) + pltpu.roll(here, 31, 1)
            pace = rates[pl.ds(i, 2)]
            pace = jnp.concatenate([pace, pace], axis=2)
            new[pl.ds(i, 2)] = here + pace * (beside - 4.0 * here)
            return carry

        lax.fori_loop(0, 12 - step, advance, 0)
        old, new = new, old

    for copy in first_x:
        copy.wait_recv()
    total = half[x, :, :, 0:XF].astype(F32)
    for dx in range(1, NX):
        total = total + x1[dx].astype(F32)
    sum_x[...] = total
    out_x[...] = total.astype(BF16)
    last_z = [
        remote(out_x.at[(z + dz) % NZ], z2.at[dz], z2_send.at[dz], z2_recv.at[dz], at_z(dz)) for dz in FAR_Z
    ]
    for copy in last_z:
        copy.start()
    for copy in first_z:
        copy.wait_recv()
    total = half[:, z, :, XF:].astype(F32)
    for dz in range(1, NZ):
        total = total + z1[dz].astype(F32)
    sum_z[...] = total
    out_z[...] = total.astype(BF16)
    last_x = [
        remote(out_z.at[(x + dx) % NX], x2.at[dx], x2_send.at[dx], x2_recv.at[dx], at_x(dx)) for dx in FAR_X
    ]
    for copy in last_x:
        copy.start()

    for t in SENDING:
        homeward[t].wait_recv()
    square = iota((COLUMNS, COLUMNS), 0) == iota((COLUMNS, COLUMNS), 1)
    tall = jnp.where(square, jnp.broadcast_to(places_ref[...], (COLUMNS, COLUMNS)), 0.0)
    tall = jnp.sum(tall, axis=1, keepdims=True).astype(I32)
    picking = jnp.where(iota((COLUMNS, SLOTS * CAP), 1) == tall, 1.0, 0.0).astype(BF16)
    tend = jnp.dot(
        picking, home[:, :, 0:FEATS].reshape(SLOTS * CAP, FEATS), preferred_element_type=F32
    )
    new_ref[...] = old[4:20, 8:24] + 0.5 * tend.reshape(SIDE, SIDE, FEATS)
    adjoint = jnp.dot(
        picking, home[:, :, FEATS:].reshape(SLOTS * CAP, FEATS), preferred_element_type=F32
    )
    adj_ref[...] = adjoint.astype(BF16).reshape(SIDE, SIDE, FEATS)

    for copy in last_z:
        copy.wait_recv()
    total = sum_x[z]
    for dz in range(1, NZ):
        total = total + z2[dz].astype(F32)
    for h in range(0, XF, 128):
        grad_ref[pl.ds(h // 128, 8, stride=8), :] = total[:, h : h + 128]
    for copy in last_x:
        copy.wait_recv()
    total = sum_z[x]
    for dx in range(1, NX):
        total = total + x2[dx].astype(F32)
    for h in range(XF, HID, 128):
        grad_ref[pl.ds(h // 128, 8, stride=8), :] = total[:, h - XF : h - XF + 128]

    for t in SENDING:
        fwd[t].wait_send()
        homeward[t].wait_send()
    for copy in edges + paces + pairs + first_x + first_z + last_x + last_z:
        copy.wait_send()


def put_out(*refs):
    copies = [pltpu.make_async_copy(refs[n], refs[3 + n], refs[6].at[n]) for n in range(3)]
    for copy in copies:
        copy.start()
    for copy in copies:
        copy.wait()


def local(state, rate, cotangent, dest, w_in, w_out):
    vmem = pl.BlockSpec(memory_space=pltpu.VMEM)
    hbm = pl.BlockSpec(memory_space=pl.ANY)
    sems = pltpu.SemaphoreType.DMA
    results = pl.pallas_call(
        kernel,
        out_shape=(
            pltpu.VMEM((SIDE, SIDE, FEATS), F32),
            pltpu.VMEM((SIDE, SIDE, FEATS), BF16),
            pltpu.VMEM((HID // 128 * 8, 128), F32),
        ),
        in_specs=[hbm] * 6,
        out_specs=(vmem, vmem, vmem),
        scratch_shapes=[
            pltpu.VMEM((SIDE, SIDE, FEATS), F32),
            pltpu.VMEM((SIDE, SIDE), F32),
            pltpu.VMEM((SIDE, SIDE, FEATS), BF16),
            pltpu.VMEM((1, COLUMNS), I32),
            pltpu.VMEM((FEATS, HID), BF16),
            pltpu.VMEM((FEATS, HID), BF16),
            pltpu.VMEM((SLOTS, CAP, 2 * FEATS), BF16),
            pltpu.VMEM((SLOTS, CAP, 2 * FEATS), BF16),
            pltpu.VMEM((SLOTS, CAP, 2 * FEATS), BF16),
            pltpu.VMEM((SLOTS, CAP, 2 * FEATS), BF16),
            pltpu.VMEM((1, COLUMNS), F32),
            pltpu.VMEM((SLOTS * CAP, HID), BF16),
            pltpu.VMEM((SLOTS * CAP, HID), BF16),
            pltpu.VMEM((SIDE, 2, 8, FEATS), BF16),
            pltpu.VMEM((24, 4, 8, FEATS), BF16),
            pltpu.VMEM((SIDE, 128), F32),
            pltpu.VMEM((8, SIDE, 128), F32),
            pltpu.VMEM((24, 32, FEATS), F32),
            pltpu.VMEM((24, 32, FEATS), F32),
            pltpu.VMEM((24, 32, 128), F32),
            pltpu.VMEM((32, 2, 8, HID), PAIR),
            pltpu.VMEM((32, 8, HID), PAIR),
            pltpu.VMEM((NX, NZ, 8, HID), BF16),
            pltpu.VMEM((NX, NZ, 8, XF), BF16),
            pltpu.VMEM((NZ, NX, 8, HID - XF), BF16),
            pltpu.VMEM((NZ, 8, XF), F32),
            pltpu.VMEM((NZ, 8, XF), BF16),
            pltpu.VMEM((NZ, 8, XF), BF16),
            pltpu.VMEM((NX, 8, HID - XF), F32),
            pltpu.VMEM((NX, 8, HID - XF), BF16),
            pltpu.VMEM((NX, 8, HID - XF), BF16),
            sems((6,)),
            sems((SLOTS,)),
            sems((SLOTS,)),
            sems((SLOTS,)),
            sems((SLOTS,)),
            sems((8,)),
            sems((8,)),
            sems((8,)),
            sems((8,)),
            sems((2,)),
            sems((2,)),
            sems((NX,)),
            sems((NX,)),
            sems((NZ,)),
            sems((NZ,)),
            sems((NX,)),
            sems((NX,)),
            sems((NZ,)),
            sems((NZ,)),
        ],
        compiler_params=pltpu.CompilerParams(collective_id=0, has_side_effects=True),
        name="window",
    )(state, rate, cotangent, dest.reshape(1, COLUMNS), w_in[0], w_out[0])
    new_state, adjoint, grads = pl.pallas_call(
        put_out,
        out_shape=(
            jax.ShapeDtypeStruct((SIDE, SIDE, FEATS), F32),
            jax.ShapeDtypeStruct((SIDE, SIDE, FEATS), BF16),
            jax.ShapeDtypeStruct((HID // 128 * 8, 128), F32),
        ),
        in_specs=[vmem] * 3,
        out_specs=(hbm,) * 3,
        scratch_shapes=[sems((3,))],
        name="put_out",
    )(*(pltpu.with_memory_space_constraint(r, pltpu.VMEM) for r in results))
    return new_state, adjoint, grads[None]


def solution(mesh):
    in_specs = (
        P("row", ("grp", "col"), None),
        P("row", ("grp", "col")),
        P("row", ("grp", "col"), None),
        P("row", ("grp", "col"), None, None),
        P("grp", None, None),
        P("grp", None, None),
    )
    out_specs = (
        P("row", ("grp", "col"), None),
        P("row", ("grp", "col"), None),
        P("grp", ("row", "col"), None),
    )
    return jax.shard_map(local, mesh=mesh, in_specs=in_specs, out_specs=out_specs, check_vma=False)
```

```python
import jax
import jax.numpy as jnp
from jax import lax
from jax.experimental import pallas as pl
from jax.experimental.pallas import tpu as pltpu
from jax.sharding import PartitionSpec as P

F32, BF16, I32 = jnp.float32, jnp.bfloat16, jnp.int32
MESH = pl.DeviceIdType.MESH

STEPS = 4
SIDE = 16
FEATS = 256
HID = 1024
CAP = 32
ROWS, BLOCKS = 32, 32
NX, NZ = 8, 4
NY, NL = 8, 2
SLOTS = NY * NL
COLUMNS = SIDE * SIDE
XF = 640
TN = 256

OFFSETS = sorted(
    ((dy, dl) for dy in range(NY) for dl in range(NL)),
    key=lambda o: 4 * ((4 - min(o[0], 8 - o[0])) % 4) + 2 * (o[0] >= 4) + o[1],
)
SENDING = [2, 3, 1] + list(range(4, SLOTS))
SIDES = [(0, 1), (0, -1), (1, 0), (-1, 0), (1, 1), (1, -1), (-1, 1), (-1, -1)]
FAR_X = [4, 3, 5, 2, 6, 1, 7]
FAR_Z = [2, 1, 3]
PAIR = BF16


def iota(shape, dim):
    return lax.broadcasted_iota(I32, shape, dim)


def kernel(
    state_hbm,
    rate_hbm,
    cot_hbm,
    dest_hbm,
    win_hbm,
    wout_hbm,
    new_ref,
    adj_ref,
    grad_ref,
    state_ref,
    rate_ref,
    cot_ref,
    dest_ref,
    win,
    wout,
    send,
    recv,
    back,
    home,
    places_ref,
    act_ref,
    dpre_ref,
    edge,
    halo,
    pace_out,
    pace_in,
    field_a,
    field_b,
    rates,
    grads,
    pair,
    half,
    x1,
    z1,
    sum_x,
    out_x,
    z2,
    sum_z,
    out_z,
    x2,
    in_sem,
    fwd_send,
    fwd_recv,
    back_send,
    back_recv,
    edge_send,
    edge_recv,
    pace_send,
    pace_recv,
    pair_send,
    pair_recv,
    x1_send,
    x1_recv,
    z1_send,
    z1_recv,
    x2_send,
    x2_recv,
    z2_send,
    z2_recv,
):
    row, grp, col = lax.axis_index("row"), lax.axis_index("grp"), lax.axis_index("col")
    x, z = row // NZ, row % NZ
    y, l = grp // NL, grp % NL
    block = grp * 2 + col

    def at_expert(dy, dl):
        return {"row": row, "grp": ((y + dy) % NY) * NL + (l + dl) % NL, "col": col}

    def at_source(dy, dl):
        return {"row": row, "grp": ((y + NY - dy) % NY) * NL + (l + dl) % NL, "col": col}

    def at_side(di, dj):
        there = (block + dj + BLOCKS) % BLOCKS
        return {"row": (row + di + ROWS) % ROWS, "grp": there // 2, "col": there % 2}

    def at_x(dx):
        return {"row": ((x + dx) % NX) * NZ + z, "grp": grp, "col": col}

    def at_z(dz):
        return {"row": x * NZ + (z + dz) % NZ, "grp": grp, "col": col}

    partner = {"row": row, "grp": grp, "col": 1 - col}

    loads = [
        pltpu.make_async_copy(src, dst, in_sem.at[n])
        for n, (src, dst) in enumerate(
            (
                (dest_hbm, dest_ref),
                (state_hbm, state_ref),
                (cot_hbm, cot_ref),
                (rate_hbm, rate_ref),
                (win_hbm, win),
                (wout_hbm, wout),
            )
        )
    ]
    for copy in loads:
        copy.start()

    barrier = pltpu.get_barrier_semaphore()
    greeted = (
        [at_expert(*OFFSETS[t]) for t in SENDING]
        + [at_side(*o) for o in SIDES]
        + [at_x(dx) for dx in FAR_X]
        + [at_z(dz) for dz in FAR_Z]
        + [partner]
    )
    for there in greeted:
        pl.semaphore_signal(barrier, inc=1, device_id=there, device_id_type=MESH)

    def remote(src, dst, sent, came, there):
        return pltpu.make_async_remote_copy(
            src_ref=src, dst_ref=dst, send_sem=sent, recv_sem=came, device_id=there, device_id_type=MESH
        )

    loads[0].wait()

    dest = dest_ref[...]
    dy = ((dest >> 1) - y) & (NY - 1)
    dl = (dest & 1) ^ l
    slot = ((4 - jnp.minimum(dy, NY - dy)) & 3) * 4 + jnp.where(dy >= 4, 2, 0) + dl
    chosen = jnp.where(iota((SLOTS, COLUMNS), 0) == slot, 1.0, 0.0)
    upto = jnp.where(
        iota((COLUMNS, COLUMNS), 0) <= iota((COLUMNS, COLUMNS), 1), 1.0, 0.0
    ).astype(BF16)
    ranks = jnp.dot(chosen.astype(BF16), upto, preferred_element_type=F32)
    rank = jnp.sum(chosen * ranks, axis=0, keepdims=True) - 1.0
    places = slot.astype(F32) * CAP + rank
    places_ref[...] = places
    placing = jnp.where(
        iota((SLOTS * CAP, COLUMNS), 0) == places.astype(I32), 1.0, 0.0
    ).astype(BF16)
    loads[1].wait()
    cells = state_ref[...].astype(BF16)
    packed = jnp.dot(placing, cells.reshape(COLUMNS, FEATS), preferred_element_type=F32)
    packed = packed.astype(BF16).reshape(SLOTS, CAP, FEATS)
    send[:, :, 0:FEATS] = packed
    recv[0, :, 0:FEATS] = packed[0]
    loads[2].wait()
    packed = 0.5 * jnp.dot(
        placing, cot_ref[...].reshape(COLUMNS, FEATS), preferred_element_type=F32
    )
    packed = packed.astype(BF16).reshape(SLOTS, CAP, FEATS)
    send[:, :, FEATS:] = packed
    recv[0, :, FEATS:] = packed[0]

    pl.semaphore_wait(barrier, len(greeted))

    fwd = {
        t: remote(send.at[t], recv.at[t], fwd_send.at[t], fwd_recv.at[t], at_expert(*OFFSETS[t]))
        for t in SENDING
    }
    for t in SENDING[:3]:
        fwd[t].start()

    loads[3].wait()
    edge[...] = cells.reshape(SIDE, 2, 8, FEATS)
    pace_out[...] = jnp.zeros_like(pace_out)
    pace_out[:, 0:SIDE] = rate_ref[...]

    span = {-1: (slice(0, 4), slice(20, 24)), 1: (slice(12, 16), slice(0, 4)), 0: (slice(0, 16), slice(4, 20))}
    tile = {-1: (slice(0, 1), slice(3, 4)), 1: (slice(1, 2), slice(0, 1)), 0: (slice(0, 2), slice(1, 3))}
    edges = [
        remote(
            edge.at[span[di][0], tile[dj][0]],
            halo.at[span[di][1], tile[dj][1]],
            edge_send.at[n],
            edge_recv.at[n],
            at_side(di, dj),
        )
        for n, (di, dj) in enumerate(SIDES)
    ]
    paces = [
        remote(pace_out, pace_in.at[n], pace_send.at[n], pace_recv.at[n], at_side(*o))
        for n, o in enumerate(SIDES)
    ]
    for t in SENDING[3:]:
        fwd[t].start()
    for copy in edges + paces:
        copy.start()

    for copy in loads[4:]:
        copy.wait()

    homeward = {
        t: remote(back.at[t], home.at[t], back_send.at[t], back_recv.at[t], at_source(*OFFSETS[t]))
        for t in SENDING
    }
    def spread(line, first, i, j, width):
        own = iota((width, 128), 1) == iota((width, 128), 0) + first
        line = jnp.where(own, jnp.broadcast_to(line, (width, 128)), 0.0)
        line = jnp.sum(line, axis=1, keepdims=True)
        rates[i, j : j + width, :] = jnp.broadcast_to(line, (width, 128))

    def answer(g):
        lines = slice(128 * g, 128 * g + 128)
        across = (((1,), (1,)), ((), ()))
        tend = lax.dot_general(act_ref[lines, :], wout[...], across, preferred_element_type=F32)
        adjoint = lax.dot_general(dpre_ref[lines, :], win[...], across, preferred_element_type=F32)
        tend = tend.astype(BF16).reshape(4, CAP, FEATS)
        adjoint = adjoint.astype(BF16).reshape(4, CAP, FEATS)
        back[4 * g : 4 * g + 4, :, 0:FEATS] = tend
        back[4 * g : 4 * g + 4, :, FEATS:] = adjoint
        if g == 0:
            home[0, :, 0:FEATS] = tend[0]
            home[0, :, FEATS:] = adjoint[0]

    for g in range(4):
        for t in range(4 * g, 4 * g + 4):
            if t:
                fwd[t].wait_recv()
        if g >= 2:
            for t in SENDING[3 * g - 6 : 8 * g - 13]:
                homeward[t].start()
        lines = slice(128 * g, 128 * g + 128)
        came = recv[4 * g : 4 * g + 4].reshape(128, 2 * FEATS)
        columns, dtend = came[:, 0:FEATS], came[:, FEATS:]
        for h in range(0, HID, TN):
            pre = jnp.dot(columns, win[:, h : h + TN], preferred_element_type=F32)
            dact = jnp.dot(dtend, wout[:, h : h + TN], preferred_element_type=F32)
            sigma = 1.0 / (1.0 + jnp.exp(-pre))
            act_ref[lines, h : h + TN] = (pre * sigma).astype(BF16)
            slope = sigma * (1.0 + pre * (1.0 - sigma))
            dpre_ref[lines, h : h + TN] = (dact * slope).astype(BF16)
        if g < 3:
            answer(g)

    parts = (slice(0, XF), slice(XF, HID))
    pairs = []
    for n, part in enumerate(parts):
        for first, hidden, out in ((FEATS, act_ref, slice(16, 32)), (0, dpre_ref, slice(0, 16))):
            left = recv[:, :, first : first + FEATS].reshape(SLOTS * CAP, FEATS)
            for h in range(part.start, part.stop, TN):
                width = min(TN, part.stop - h)
                piece = lax.dot_general(
                    left, hidden[:, h : h + width], (((0,), (0,)), ((), ())), preferred_element_type=F32
                )
                grads[out, :, :, h : h + width] = piece.reshape(16, 2, 8, width).astype(PAIR)
        copy = remote(
            grads.at[:, 1 - col, :, part], pair.at[:, :, part], pair_send.at[n], pair_recv.at[n], partner
        )
        copy.start()
        pairs.append(copy)
    answer(3)
    for t in SENDING[11:]:
        homeward[t].start()
    first_x = [
        remote(
            half.at[(x + dx) % NX, :, :, 0:XF], x1.at[dx], x1_send.at[dx], x1_recv.at[dx], at_x(dx)
        )
        for dx in FAR_X
    ]
    first_z = [
        remote(
            half.at[:, (z + dz) % NZ, :, XF:], z1.at[dz], z1_send.at[dz], z1_recv.at[dz], at_z(dz)
        )
        for dz in FAR_Z
    ]
    for part, copy, onward in zip(parts, pairs, (first_x, first_z)):
        copy.wait_recv()
        both = grads[:, col, :, part].astype(F32) + pair[:, :, part].astype(F32)
        half[:, :, :, part] = both.astype(BF16).reshape(NX, NZ, 8, part.stop - part.start)
        for there in onward:
            there.start()

    for i in range(SIDE):
        spread(pace_out[i : i + 1, :], 0, 4 + i, 8, SIDE)
    for copy in edges + paces:
        copy.wait_recv()
    for n, (di, dj) in enumerate(SIDES):
        (source, target), (left, right) = span[di], tile[dj]
        for i in range(target.stop - target.start):
            spread(
                pace_in[n, source.start + i : source.start + i + 1, :],
                8 * left.start,
                target.start + i,
                8 * right.start,
                8 * (right.stop - right.start),
            )
    for top in (0, 20):
        field_a[top : top + 4] = halo[top : top + 4].astype(F32).reshape(4, 32, FEATS)
    for t in (0, 3):
        field_a[4:20, 8 * t : 8 * t + 8] = halo[4:20, t].astype(F32)
    field_a[4:20, 8:24] = state_ref[...]
    old, new = field_a, field_b
    for step in range(1, STEPS + 1):

        def advance(n, carry, old=old, new=new, step=step):
            i = step + 2 * n
            here = old[pl.ds(i, 2)]
            beside = old[pl.ds(i - 1, 2)] + old[pl.ds(i + 1, 2)]
            beside = beside + pltpu.roll(here, 1, 1) + pltpu.roll(here, 31, 1)
            pace = rates[pl.ds(i, 2)]
            pace = jnp.concatenate([pace, pace], axis=2)
            new[pl.ds(i, 2)] = here + pace * (beside - 4.0 * here)
            return carry

        lax.fori_loop(0, 12 - step, advance, 0)
        old, new = new, old

    for copy in first_x:
        copy.wait_recv()
    total = half[x, :, :, 0:XF].astype(F32)
    for dx in range(1, NX):
        total = total + x1[dx].astype(F32)
    sum_x[...] = total
    out_x[...] = total.astype(BF16)
    last_z = [
        remote(out_x.at[(z + dz) % NZ], z2.at[dz], z2_send.at[dz], z2_recv.at[dz], at_z(dz)) for dz in FAR_Z
    ]
    for copy in last_z:
        copy.start()
    for copy in first_z:
        copy.wait_recv()
    total = half[:, z, :, XF:].astype(F32)
    for dz in range(1, NZ):
        total = total + z1[dz].astype(F32)
    sum_z[...] = total
    out_z[...] = total.astype(BF16)
    last_x = [
        remote(out_z.at[(x + dx) % NX], x2.at[dx], x2_send.at[dx], x2_recv.at[dx], at_x(dx)) for dx in FAR_X
    ]
    for copy in last_x:
        copy.start()

    for t in SENDING:
        homeward[t].wait_recv()
    square = iota((COLUMNS, COLUMNS), 0) == iota((COLUMNS, COLUMNS), 1)
    tall = jnp.where(square, jnp.broadcast_to(places_ref[...], (COLUMNS, COLUMNS)), 0.0)
    tall = jnp.sum(tall, axis=1, keepdims=True).astype(I32)
    picking = jnp.where(iota((COLUMNS, SLOTS * CAP), 1) == tall, 1.0, 0.0).astype(BF16)
    tend = jnp.dot(
        picking, home[:, :, 0:FEATS].reshape(SLOTS * CAP, FEATS), preferred_element_type=F32
    )
    new_ref[...] = old[4:20, 8:24] + 0.5 * tend.reshape(SIDE, SIDE, FEATS)
    adjoint = jnp.dot(
        picking, home[:, :, FEATS:].reshape(SLOTS * CAP, FEATS), preferred_element_type=F32
    )
    adj_ref[...] = adjoint.astype(BF16).reshape(SIDE, SIDE, FEATS)

    for copy in last_z:
        copy.wait_recv()
    total = sum_x[z]
    for dz in range(1, NZ):
        total = total + z2[dz].astype(F32)
    for h in range(0, XF, 128):
        grad_ref[pl.ds(h // 128, 8, stride=8), :] = total[:, h : h + 128]
    for copy in last_x:
        copy.wait_recv()
    total = sum_z[x]
    for dx in range(1, NX):
        total = total + x2[dx].astype(F32)
    for h in range(XF, HID, 128):
        grad_ref[pl.ds(h // 128, 8, stride=8), :] = total[:, h - XF : h - XF + 128]

    for t in SENDING:
        fwd[t].wait_send()
        homeward[t].wait_send()
    for copy in edges + paces + pairs + first_x + first_z + last_x + last_z:
        copy.wait_send()


def put_out(*refs):
    copies = [pltpu.make_async_copy(refs[n], refs[3 + n], refs[6].at[n]) for n in range(3)]
    for copy in copies:
        copy.start()
    for copy in copies:
        copy.wait()


def local(state, rate, cotangent, dest, w_in, w_out):
    vmem = pl.BlockSpec(memory_space=pltpu.VMEM)
    hbm = pl.BlockSpec(memory_space=pl.ANY)
    sems = pltpu.SemaphoreType.DMA
    results = pl.pallas_call(
        kernel,
        out_shape=(
            pltpu.VMEM((SIDE, SIDE, FEATS), F32),
            pltpu.VMEM((SIDE, SIDE, FEATS), BF16),
            pltpu.VMEM((HID // 128 * 8, 128), F32),
        ),
        in_specs=[hbm] * 6,
        out_specs=(vmem, vmem, vmem),
        scratch_shapes=[
            pltpu.VMEM((SIDE, SIDE, FEATS), F32),
            pltpu.VMEM((SIDE, SIDE), F32),
            pltpu.VMEM((SIDE, SIDE, FEATS), BF16),
            pltpu.VMEM((1, COLUMNS), I32),
            pltpu.VMEM((FEATS, HID), BF16),
            pltpu.VMEM((FEATS, HID), BF16),
            pltpu.VMEM((SLOTS, CAP, 2 * FEATS), BF16),
            pltpu.VMEM((SLOTS, CAP, 2 * FEATS), BF16),
            pltpu.VMEM((SLOTS, CAP, 2 * FEATS), BF16),
            pltpu.VMEM((SLOTS, CAP, 2 * FEATS), BF16),
            pltpu.VMEM((1, COLUMNS), F32),
            pltpu.VMEM((SLOTS * CAP, HID), BF16),
            pltpu.VMEM((SLOTS * CAP, HID), BF16),
            pltpu.VMEM((SIDE, 2, 8, FEATS), BF16),
            pltpu.VMEM((24, 4, 8, FEATS), BF16),
            pltpu.VMEM((SIDE, 128), F32),
            pltpu.VMEM((8, SIDE, 128), F32),
            pltpu.VMEM((24, 32, FEATS), F32),
            pltpu.VMEM((24, 32, FEATS), F32),
            pltpu.VMEM((24, 32, 128), F32),
            pltpu.VMEM((32, 2, 8, HID), PAIR),
            pltpu.VMEM((32, 8, HID), PAIR),
            pltpu.VMEM((NX, NZ, 8, HID), BF16),
            pltpu.VMEM((NX, NZ, 8, XF), BF16),
            pltpu.VMEM((NZ, NX, 8, HID - XF), BF16),
            pltpu.VMEM((NZ, 8, XF), F32),
            pltpu.VMEM((NZ, 8, XF), BF16),
            pltpu.VMEM((NZ, 8, XF), BF16),
            pltpu.VMEM((NX, 8, HID - XF), F32),
            pltpu.VMEM((NX, 8, HID - XF), BF16),
            pltpu.VMEM((NX, 8, HID - XF), BF16),
            sems((6,)),
            sems((SLOTS,)),
            sems((SLOTS,)),
            sems((SLOTS,)),
            sems((SLOTS,)),
            sems((8,)),
            sems((8,)),
            sems((8,)),
            sems((8,)),
            sems((2,)),
            sems((2,)),
            sems((NX,)),
            sems((NX,)),
            sems((NZ,)),
            sems((NZ,)),
            sems((NX,)),
            sems((NX,)),
            sems((NZ,)),
            sems((NZ,)),
        ],
        compiler_params=pltpu.CompilerParams(collective_id=0, has_side_effects=True),
        name="window",
    )(state, rate, cotangent, dest.reshape(1, COLUMNS), w_in[0], w_out[0])
    new_state, adjoint, grads = pl.pallas_call(
        put_out,
        out_shape=(
            jax.ShapeDtypeStruct((SIDE, SIDE, FEATS), F32),
            jax.ShapeDtypeStruct((SIDE, SIDE, FEATS), BF16),
            jax.ShapeDtypeStruct((HID // 128 * 8, 128), F32),
        ),
        in_specs=[vmem] * 3,
        out_specs=(hbm,) * 3,
        scratch_shapes=[sems((3,))],
        name="put_out",
    )(*(pltpu.with_memory_space_constraint(r, pltpu.VMEM) for r in results))
    return new_state, adjoint, grads[None]


def solution(mesh):
    in_specs = (
        P("row", ("grp", "col"), None),
        P("row", ("grp", "col")),
        P("row", ("grp", "col"), None),
        P("row", ("grp", "col"), None, None),
        P("grp", None, None),
        P("grp", None, None),
    )
    out_specs = (
        P("row", ("grp", "col"), None),
        P("row", ("grp", "col"), None),
        P("grp", ("row", "col"), None),
    )
    return jax.shard_map(local, mesh=mesh, in_specs=in_specs, out_specs=out_specs, check_vma=False)
```
